32 devices in a mesh: fsdp: 8 (over y, x, core), ulysses: 4 (over z).
Axes of the slice: x: 2, y: 2, z: 4, core: 2. Of those that a mesh axis runs over, the one named last changes fastest.
Arguments:
- layer_input: bfloat16 [24, 1024, 2048], P('fsdp', 'ulysses'), may hold values from -6 to 6
- cotangent: bfloat16 [24, 1024, 2048], P('fsdp', 'ulysses'), may hold values from -6 to 6
- positions: int32 [24, 1024], P('fsdp', 'ulysses'), may hold values from 0 to 4095
- block_ids: int32 [24, 1024], P('fsdp'), may hold values from 0 to 7, never falling along the last dimension, each value on 1 to 256 neighbouring positions
- skip_mask: int32 [24], P('fsdp'), may hold values 0 or 1
- attn_gain: bfloat16 [2048], P('fsdp'), may hold values from 0.5 to 1.5
- w_query: bfloat16 [2048, 2048], P('fsdp'), may hold values from -0.125 to 0.125
- w_key: bfloat16 [2048, 512], P('fsdp'), may hold values from -0.125 to 0.125
- w_value: bfloat16 [2048, 512], P('fsdp'), may hold values from -0.125 to 0.125
- w_out: bfloat16 [2048, 2048], P('fsdp'), may hold values from -1 to 1
- mlp_gain: bfloat16 [2048], P('fsdp'), may hold values from 0.5 to 1.5
- w_gate: bfloat16 [2048, 5632], P('fsdp'), may hold values from -0.125 to 0.125
- w_up: bfloat16 [2048, 5632], P('fsdp'), may hold values from -0.125 to 0.125
- w_down: bfloat16 [5632, 2048], P(None, 'fsdp'), may hold values from -0.078125 to 0.078125
Outputs:
- output: bfloat16 [24, 1024, 2048], P('fsdp', 'ulysses')
- grad_input: bfloat16 [24, 1024, 2048], P('fsdp', 'ulysses')
- grad_attn_gain: float32 [2048], P('fsdp')
- grad_w_query: float32 [2048, 2048], P('fsdp')
- grad_w_key: float32 [2048, 512], P('fsdp')
- grad_w_value: float32 [2048, 512], P('fsdp')
- grad_w_out: float32 [2048, 2048], P('fsdp')
- grad_mlp_gain: float32 [2048], P('fsdp')
- grad_w_gate: float32 [2048, 5632], P('fsdp')
- grad_w_up: float32 [2048, 5632], P('fsdp')
- grad_w_down: float32 [5632, 2048], P(None, 'fsdp')
The draws below stay inside these ranges and needn't reach their ends.
Inputs may be any that keep to these rules, and one draw needn't show every extreme that they name: `block_ids`: within a sequence block numbers never fall, every number of 0 to 7 occurs, and a block has 1 to 256 tokens.
All inputs are finite; a program needn't handle non-finite values. No bound on the sum of `skip_mask` on one device may be relied on, other than what follows from the above.
Results may differ from the reference program's by a relative error of at most 0.022.
Values may be sent and summed in bfloat16 or wider, within the bound.
No kernel may reach another device: no remote copies, remote signals or barrier semaphores. Data moves between devices by JAX's collectives and lax.ppermute only.
A program may use at most 640 MiB of HBM per device.

```python
import math
import jax
import jax.numpy as jnp
import numpy as np
from jax import lax

D = 2048
H = 16
KVH = 4
HD = 128
FF = 5632
LEN = 1024
BLOCK = 256
NBLK = 8
SEQS = 24
N_ULYSSES = 4


def plant(array, stream_key, smallest, top_value):
    extent = array.shape
    place = [jax.random.randint(jax.random.fold_in(stream_key, axis), (), 0, extent[axis]) for axis in range(len(extent))]
    array = array.at[tuple(place)].set(smallest)
    longest = extent.index(max(extent))
    place[longest] = (place[longest] + 1) % extent[longest]
    return array.at[tuple(place)].set(top_value)


def level_of(own_key, extent, split, low, high):
    def one(position, blocks):
        draws = jax.random.uniform(jax.random.fold_in(jax.random.fold_in(own_key, 6), position), (blocks,), jnp.float32, low / len(split), high / len(split))
        return jnp.repeat(jnp.exp(draws), extent[position] // blocks).reshape((-1,) + (1,) * (len(extent) - position - 1))

    loudness = one(*split[0])
    for cut in split[1:]:
        loudness = loudness * one(*cut)
    return loudness


def profile(number_of, total, most, lean):
    loads = [(1 << 20) // math.isqrt(rank ** lean) + 1 for rank in range(2, number_of + 1)]
    surplus, given = total - most - (number_of - 1), [1] * (number_of - 1)
    while surplus > 0:
        candidates = [i for i in range(number_of - 1) if given[i] < most]
        pool, left = sum([loads[i] for i in candidates]), surplus
        for i in candidates:
            extra = min(most - given[i], max(1, left * loads[i] // pool), surplus)
            given[i] = given[i] + extra
            surplus = surplus - extra
    return np.array([most] + given)


def ragged(stream_key, amount, total, bound, slope):
    if amount == 2:
        one = jax.random.randint(stream_key, (), max(1, total - bound), min(bound, total - 1) + 1)
        return jnp.stack([one, total - one])
    sizes = jnp.asarray(profile(amount, total, bound, slope), jnp.int32)
    pairs = (amount - 1) // 2
    donor, receiver = sizes[1:1 + 2 * pairs:2], sizes[2:2 + 2 * pairs:2]
    room = jnp.minimum(donor - 1, bound - receiver)
    passed = jax.random.randint(jax.random.fold_in(stream_key, 1), (pairs,), 0, 1 << 20) % (room + 1)
    sizes = sizes.at[1:1 + 2 * pairs:2].set(donor - passed).at[2:2 + 2 * pairs:2].set(receiver + passed)
    return sizes[jax.random.permutation(jax.random.fold_in(stream_key, 2), amount)]


def noise(own_key, dims, width, most, pieces=(), held_as=jnp.bfloat16):
    level = level_of(own_key, dims, pieces, -0.22, 0.18) if pieces else 1.0
    drawn = jax.random.normal(own_key, dims, jnp.float32) * width * level
    return jnp.minimum(jnp.maximum(drawn, -most), most).astype(held_as)


def setup_inputs(seed: int = 0) -> dict:
    splits = jax.random.split(jax.random.key(seed), 15)
    return {
        "layer_input": noise(splits[0], (SEQS, LEN, D), 1.0, 6.0, ((0, 8), (1, 4))),
        "cotangent": noise(splits[1], (SEQS, LEN, D), 1.0, 6.0, ((0, 8), (1, 4))),
        "positions": plant(jax.random.randint(splits[2], (SEQS, LEN), 0, 4 * LEN), jax.random.fold_in(splits[2], 1), 0, (4 * LEN) - 1).astype(jnp.int32),
        "block_ids": jax.vmap(lambda own: jnp.searchsorted(jnp.cumsum(ragged(own, NBLK, LEN, BLOCK, 0)), jnp.arange(LEN), side="right"))(jax.random.split(splits[3], SEQS)).reshape((SEQS, LEN)).astype(jnp.int32),
        "skip_mask": plant((jax.random.randint(splits[4], (SEQS,), 0, 4) < 1).astype(jnp.int32), jax.random.fold_in(splits[4], 1), 0, 1),
        "attn_gain": jnp.clip(1.0 + 0.1 * jax.random.normal(splits[5], (D,), jnp.float32), 0.5, 1.5).astype(jnp.bfloat16),
        "w_query": noise(splits[6], (D, H * HD), D ** -0.5, 0.125, ((0, 8),)),
        "w_key": noise(splits[7], (D, KVH * HD), D ** -0.5, 0.125, ((0, 8),)),
        "w_value": noise(splits[8], (D, KVH * HD), D ** -0.5, 0.125, ((0, 8),)),
        "w_out": noise(splits[9], (H * HD, D), (H * HD // 64) ** -0.5, 1.0, ((0, 8),)),
        "mlp_gain": jnp.clip(1.0 + 0.1 * jax.random.normal(splits[10], (D,), jnp.float32), 0.5, 1.5).astype(jnp.bfloat16),
        "w_gate": noise(splits[11], (D, FF), D ** -0.5, 0.125, ((0, 8),)),
        "w_up": noise(splits[12], (D, FF), D ** -0.5, 0.125, ((0, 8),)),
        "w_down": noise(splits[13], (FF, D), FF ** -0.5, 0.078125, ((1, 8),)),
    }


@jax.custom_vjp
def low(v):
    return lax.optimization_barrier(v.astype(jnp.bfloat16)).astype(jnp.float32)

@jax.custom_vjp
def low_back(v):
    return v

def low_keep(v):
    return (low(v), None)

def low_pass(kept, grad):
    return (grad,)

def back_keep(v):
    return (v, None)

def back_low(kept, grad):
    return (low(grad),)
low.defvjp(low_keep, low_pass)
low_back.defvjp(back_keep, back_low)
epsilon = 1e-05
highest = lax.Precision.HIGHEST

def rotary_tables(token_positions):
    half_size = HD // 2
    frequency = jnp.exp(jnp.arange(half_size, dtype=jnp.float32) * (-2.0 * math.log(10000.0) / HD))
    angles = token_positions.astype(jnp.float32)[..., None] * frequency
    cosine = jnp.concatenate([jnp.cos(angles), jnp.cos(angles)], -1)
    sine_table = jnp.concatenate([jnp.sin(angles), jnp.sin(angles)], -1)
    return (cosine, sine_table)

def rotate(values, cosine, sine_table):
    half_size = values.shape[-1] // 2
    turned = jnp.concatenate([-values[..., half_size:], values[..., :half_size]], -1)
    return values * cosine[..., None, :] + turned * sine_table[..., None, :]

def layer_forward(rows_in, attn_gain, w_query, w_key, w_value, w_out, mlp_gain, w_gate, w_up, w_down, block_row, position_row, keep_value):
    repeat_count = max(1, N_ULYSSES // KVH)
    slot_count = KVH * repeat_count
    group_size = H // slot_count
    inv_one = lax.rsqrt(lax.optimization_barrier(jnp.mean(rows_in * rows_in, -1, keepdims=True)) + epsilon)
    normed_one = low(rows_in * inv_one * attn_gain)
    query_pre = low_back(jnp.dot(normed_one, w_query, precision=highest)).reshape(LEN, H, HD)
    key_pre = low_back(jnp.dot(normed_one, w_key, precision=highest)).reshape(LEN, KVH, HD)
    value_pre = low_back(jnp.dot(normed_one, w_value, precision=highest)).reshape(LEN, KVH, HD)
    cosine, sine_table = rotary_tables(position_row)
    queries = low(low_back(rotate(query_pre, cosine, sine_table)))
    keys = low(low_back(jnp.repeat(rotate(key_pre, cosine, sine_table), repeat_count, axis=1)))
    values = low(low_back(jnp.repeat(value_pre, repeat_count, axis=1)))
    grouped = queries.reshape(LEN, slot_count, group_size, HD)
    scores = low_back(jnp.einsum('qsgd,ksd->sgqk', grouped, keys, precision=highest) * (1.0 / math.sqrt(HD)))
    allowed = block_row[None, :] <= block_row[:, None]
    scores = jnp.where(allowed, scores, -1e+30)
    largest = lax.optimization_barrier(jnp.max(scores, -1, keepdims=True))
    exponent = jnp.exp(scores - largest)
    chances = low(exponent / lax.optimization_barrier(jnp.sum(exponent, -1, keepdims=True)))
    attended = jnp.einsum('sgqk,ksd->qsgd', chances, values, precision=highest).reshape(LEN, H * HD)
    attended = low(low_back(attended))
    branch_attn = low_back(jnp.dot(attended, w_out, precision=highest))
    middle = rows_in + keep_value * branch_attn
    inv_two = lax.rsqrt(lax.optimization_barrier(jnp.mean(middle * middle, -1, keepdims=True)) + epsilon)
    normed_two = low(middle * inv_two * mlp_gain)
    gate = low_back(jnp.dot(normed_two, w_gate, precision=highest))
    up_value = low_back(jnp.dot(normed_two, w_up, precision=highest))
    hidden = low(gate * jax.nn.sigmoid(gate) * up_value)
    branch_mlp = low_back(jnp.dot(hidden, w_down, precision=highest))
    return middle + keep_value * branch_mlp

def reference(layer_input, cotangent, positions, block_ids, skip_mask, attn_gain, w_query, w_key, w_value, w_out, mlp_gain, w_gate, w_up, w_down):
    weights = tuple((parameter.astype(jnp.float32) for parameter in (attn_gain, w_query, w_key, w_value, w_out, mlp_gain, w_gate, w_up, w_down)))
    keep_all = (1 - skip_mask).astype(jnp.float32)

    def one_sequence(running, record):
        rows_in, grad_rows, position_row, block_row, keep_value = record

        def apply_layer(inputs_now, *parameters):
            return layer_forward(inputs_now, *parameters, block_row, position_row, keep_value)
        result, pullback = jax.vjp(apply_layer, rows_in.astype(jnp.float32), *weights)
        gradients = pullback(grad_rows.astype(jnp.float32))
        running = tuple((total_now + grad_now for total_now, grad_now in zip(running, gradients[1:])))
        return (running, (result.astype(jnp.bfloat16), gradients[0].astype(jnp.bfloat16)))
    initial = tuple((jnp.zeros_like(parameter) for parameter in weights))
    totals, (outputs, grad_inputs) = lax.scan(one_sequence, initial, (layer_input, cotangent, positions, block_ids, keep_all))
    return (outputs, grad_inputs, totals[0], totals[1], totals[2], totals[3], totals[4], totals[5], totals[6], totals[7], totals[8])
```

```python
import math

import jax
import jax.numpy as jnp
from jax import lax
from jax.experimental import pallas as pl
from jax.experimental.pallas import tpu as pltpu
from jax.sharding import PartitionSpec as P

H = 16
KVH = 4
HD = 128
GROUP = H // KVH
BLOCK = 256
EPS = 1e-05
F32 = jnp.float32
BF16 = jnp.bfloat16
LOG2E = math.log2(math.e)

NT = (((1,), (1,)), ((), ()))
NN = (((1,), (0,)), ((), ()))


def dot(a, b, dims=NN):
    return lax.dot_general(a, b, dims, preferred_element_type=F32)


def cost(flops, nbytes, trans=0):
    return pl.CostEstimate(flops=int(flops), bytes_accessed=int(nbytes), transcendentals=int(trans))


def const_spec(shape):
    zeros = (0,) * len(shape)
    return pl.BlockSpec(shape, lambda *_: zeros)


def sds(shape, dtype):
    return jax.ShapeDtypeStruct(shape, dtype)


def project(normed, weights, cosine, sine):
    rows, width = normed.shape
    tile = KVH * HD
    steps = weights.shape[1] // tile
    q_steps = H * HD // tile

    def body(x_ref, w_ref, c_ref, s_ref, q_ref, kv_ref):
        j = pl.program_id(0)
        y = dot(x_ref[...], w_ref[...])

        def turned():
            c, s = c_ref[...], s_ref[...]
            parts = []
            for h in range(KVH):
                v = y[:, h * HD : (h + 1) * HD]
                parts.append(v * c + pltpu.roll(v, HD // 2, 1) * s)
            return jnp.concatenate(parts, 1).astype(BF16)

        @pl.when(j < q_steps)
        def _():
            q_ref[...] = turned()

        @pl.when(j == q_steps)
        def _():
            kv_ref[...] = turned()

        @pl.when(j > q_steps)
        def _():
            kv_ref[...] = y.astype(BF16)

    return pl.pallas_call(
        body,
        grid=(steps,),
        in_specs=[
            const_spec((rows, width)),
            pl.BlockSpec((width, tile), lambda j: (0, j)),
            const_spec((rows, HD)),
            const_spec((rows, HD)),
        ],
        out_specs=[
            pl.BlockSpec((rows, tile), lambda j: (0, jnp.minimum(j, q_steps - 1))),
            pl.BlockSpec((rows, tile), lambda j: (0, jnp.maximum(j - q_steps, 0))),
        ],
        out_shape=[sds((rows, H * HD), BF16), sds((rows, 2 * KVH * HD), BF16)],
        cost_estimate=cost(2 * rows * width * steps * tile, 2 * (width * steps * tile + 2 * rows * width)),
        name="project",
    )(normed, weights, cosine, sine)


def slot_specs(count, local, shift):
    return [pl.BlockSpec((local, HD), lambda s, j: (s, shift + j)) for _ in range(count)]


def attend(q, slots, block_keys, block_mine, seqs):
    rows = q.shape[0]
    local = rows // seqs
    parts = len(slots)
    full = parts * local
    scale = LOG2E / math.sqrt(HD)

    def body(q_ref, *refs):
        k_refs, v_refs = refs[:parts], refs[parts : 2 * parts]
        kid_ref, qid_ref, o_ref, lse_ref, bias_ref = refs[2 * parts :]

        @pl.when(pl.program_id(1) == 0)
        def _():
            bias_ref[...] = jnp.where(kid_ref[0] <= qid_ref[0], 0.0, -1e30)

        keys = jnp.concatenate([r[...] for r in k_refs], 0)
        values_t = jnp.concatenate([r[...] for r in v_refs], 0).T
        for h in range(GROUP):
            qh = q_ref[:, h * HD : (h + 1) * HD]
            s = dot(keys, qh, NT) * scale + bias_ref[...]
            top = jnp.max(s, 0, keepdims=True)
            e = jnp.exp2(s - top)
            total = jnp.sum(e, 0, keepdims=True)
            out_t = dot(values_t, e.astype(BF16)) * (1.0 / total)
            o_ref[:, h * HD : (h + 1) * HD] = out_t.T.astype(BF16)
            lse_ref[0, 0, h : h + 1, :] = top + jnp.log2(total)

    return pl.pallas_call(
        body,
        grid=(seqs, KVH),
        in_specs=[pl.BlockSpec((local, GROUP * HD), lambda s, j: (s, j))]
        + slot_specs(parts, local, 0)
        + slot_specs(parts, local, KVH)
        + [
            pl.BlockSpec((1, full, 1), lambda s, j: (s, 0, 0)),
            pl.BlockSpec((1, 1, local), lambda s, j: (s, 0, 0)),
        ],
        out_specs=[
            pl.BlockSpec((local, GROUP * HD), lambda s, j: (s, j)),
            pl.BlockSpec((1, 1, GROUP, local), lambda s, j: (s, j, 0, 0)),
        ],
        out_shape=[sds((rows, H * HD), BF16), sds((seqs, KVH, GROUP, local), F32)],
        scratch_shapes=[pltpu.VMEM((full, local), F32)],
        cost_estimate=cost(8 * rows * full * H * HD, 4 * rows * H * HD, rows * full * H),
        name="attend",
    )(q, *slots, *slots, block_keys, block_mine)


def attend_back(q, slots, block_keys, block_mine, lse, grad, cosine, sine, seqs):
    rows = q.shape[0]
    local = rows // seqs
    parts = len(slots)
    full = parts * local
    head_scale = 1.0 / math.sqrt(HD)
    scale = LOG2E * head_scale

    def body(q_ref, *refs):
        k_refs, v_refs = refs[:parts], refs[parts : 2 * parts]
        kid_ref, qid_ref, lse_ref, g_ref, c_ref, s_ref, dq_ref = refs[2 * parts : 2 * parts + 7]
        dkv_refs, bias_ref = refs[2 * parts + 7 : -1], refs[-1]
        j = pl.program_id(1)

        @pl.when(j == 0)
        def _():
            bias_ref[...] = jnp.where(kid_ref[0] <= qid_ref[0], 0.0, -1e30)

        keys = jnp.concatenate([r[...] for r in k_refs], 0)
        values = jnp.concatenate([r[...] for r in v_refs], 0)
        keys_t = keys.T
        c, sn = c_ref[...], s_ref[...]
        dk = jnp.zeros((full, HD), F32)
        dv = jnp.zeros((full, HD), F32)
        for h in range(GROUP):
            cols = slice(h * HD, (h + 1) * HD)
            qh = q_ref[:, cols]
            gh = g_ref[:, cols]
            p = jnp.exp2(dot(keys, qh, NT) * scale + bias_ref[...] - lse_ref[0, 0, h : h + 1, :])
            dp = dot(values, gh, NT)
            center = jnp.sum(p * dp, 0, keepdims=True)
            ds = (p * (dp - center)).astype(BF16)
            dv = dv + dot(p.astype(BF16), gh)
            dk = dk + dot(ds, qh)
            dq = dot(keys_t, ds).T * head_scale
            dq_ref[:, cols] = (dq * c + pltpu.roll(dq * sn, HD // 2, 1)).astype(BF16)
        k_at = pl.ds(pl.multiple_of(j * HD, HD), HD)
        v_at = pl.ds(pl.multiple_of((KVH + j) * HD, HD), HD)
        for part, ref in enumerate(dkv_refs):
            own = slice(part * local, (part + 1) * local)
            ref[:, k_at] = (dk[own] * head_scale).astype(BF16)
            ref[:, v_at] = dv[own].astype(BF16)

    row = lambda s, j: (s, 0)
    return pl.pallas_call(
        body,
        grid=(seqs, KVH),
        in_specs=[pl.BlockSpec((local, GROUP * HD), lambda s, j: (s, j))]
        + slot_specs(parts, local, 0)
        + slot_specs(parts, local, KVH)
        + [
            pl.BlockSpec((1, full, 1), lambda s, j: (s, 0, 0)),
            pl.BlockSpec((1, 1, local), lambda s, j: (s, 0, 0)),
            pl.BlockSpec((1, 1, GROUP, local), lambda s, j: (s, j, 0, 0)),
            pl.BlockSpec((local, GROUP * HD), lambda s, j: (s, j)),
            pl.BlockSpec((local, HD), row),
            pl.BlockSpec((local, HD), row),
        ],
        out_specs=[pl.BlockSpec((local, GROUP * HD), lambda s, j: (s, j))]
        + [pl.BlockSpec((local, 2 * KVH * HD), row)] * parts,
        out_shape=[sds((rows, H * HD), BF16)] + [sds((rows, 2 * KVH * HD), BF16)] * parts,
        scratch_shapes=[pltpu.VMEM((full, local), F32)],
        cost_estimate=cost(20 * rows * full * H * HD, 8 * rows * H * HD, rows * full * H),
        name="attend_back",
    )(q, *slots, *slots, block_keys, block_mine, lse, grad, cosine, sine)


def out_project(attended, w_out, x, keep, gain, tile):
    rows, width = x.shape
    depth = attended.shape[1]

    def body(a_ref, w_ref, x_ref, k_ref, g_ref, m_ref, n_ref):
        mid = x_ref[...].astype(F32) + k_ref[...] * dot(a_ref[...], w_ref[...])
        inv = lax.rsqrt(jnp.mean(mid * mid, -1, keepdims=True) + EPS)
        m_ref[...] = mid
        n_ref[...] = (mid * inv * g_ref[...]).astype(BF16)

    return pl.pallas_call(
        body,
        grid=(rows // tile,),
        in_specs=[
            pl.BlockSpec((tile, depth), lambda i: (i, 0)),
            const_spec((depth, width)),
            pl.BlockSpec((tile, width), lambda i: (i, 0)),
            pl.BlockSpec((tile, 1), lambda i: (i, 0)),
            const_spec((1, width)),
        ],
        out_specs=[pl.BlockSpec((tile, width), lambda i: (i, 0))] * 2,
        out_shape=[sds((rows, width), F32), sds((rows, width), BF16)],
        cost_estimate=cost(2 * rows * depth * width, 2 * depth * width + 10 * rows * width),
        name="out_project",
    )(attended, w_out, x, keep, gain)


def gate_matmul(normed, w_gate, tile):
    rows, width = normed.shape
    hidden = w_gate.shape[1]

    def body(x_ref, w_ref, g_ref):
        g_ref[...] = dot(x_ref[...], w_ref[...]).astype(BF16)

    return pl.pallas_call(
        body,
        grid=(hidden // tile,),
        in_specs=[const_spec((rows, width)), pl.BlockSpec((width, tile), lambda j: (0, j))],
        out_specs=pl.BlockSpec((rows, tile), lambda j: (0, j)),
        out_shape=sds((rows, hidden), BF16),
        cost_estimate=cost(2 * rows * width * hidden, 2 * width * hidden + 2 * rows * hidden),
        name="gate_matmul",
    )(normed, w_gate)


def up_matmul(normed, w_up, gate, tile):
    rows, width = normed.shape
    hidden = w_up.shape[1]

    def body(x_ref, w_ref, g_ref, u_ref, h_ref):
        up = dot(x_ref[...], w_ref[...])
        g = g_ref[...].astype(F32)
        u_ref[...] = up.astype(BF16)
        h_ref[...] = (g * jax.nn.sigmoid(g) * up).astype(BF16)

    return pl.pallas_call(
        body,
        grid=(hidden // tile,),
        in_specs=[
            const_spec((rows, width)),
            pl.BlockSpec((width, tile), lambda j: (0, j)),
            pl.BlockSpec((rows, tile), lambda j: (0, j)),
        ],
        out_specs=[pl.BlockSpec((rows, tile), lambda j: (0, j))] * 2,
        out_shape=[sds((rows, hidden), BF16)] * 2,
        cost_estimate=cost(2 * rows * width * hidden, 2 * width * hidden + 6 * rows * hidden, rows * hidden),
        name="up_matmul",
    )(normed, w_up, gate)


def down_matmul(hidden, w_down, middle, keep):
    rows, depth = hidden.shape
    pieces, _, tile = w_down.shape

    def body(h_ref, w_ref, m_ref, k_ref, o_ref):
        o_ref[...] = (m_ref[...] + k_ref[...] * dot(h_ref[...], w_ref[0])).astype(BF16)

    return pl.pallas_call(
        body,
        grid=(pieces,),
        in_specs=[
            const_spec((rows, depth)),
            pl.BlockSpec((1, depth, tile), lambda i: (i, 0, 0)),
            pl.BlockSpec((rows, tile), lambda i: (0, i)),
            const_spec((rows, 1)),
        ],
        out_specs=pl.BlockSpec((rows, tile), lambda i: (0, i)),
        out_shape=sds((rows, pieces * tile), BF16),
        cost_estimate=cost(2 * rows * depth * pieces * tile, 2 * depth * pieces * tile + 2 * rows * depth),
        name="down_matmul",
    )(hidden, w_down, middle, keep)


def hidden_back(grad_mlp, w_down, gate, up, tile):
    rows, width = grad_mlp.shape
    pieces, hidden, part = w_down.shape

    def body(m_ref, w_ref, g_ref, u_ref, gg_ref, gu_ref):
        acc = dot(m_ref[:, :part], w_ref[0], NT)
        for i in range(1, pieces):
            acc = acc + dot(m_ref[:, i * part : (i + 1) * part], w_ref[i], NT)
        g = g_ref[...].astype(F32)
        u = u_ref[...].astype(F32)
        sig = jax.nn.sigmoid(g)
        gg_ref[...] = (acc * u * sig * (1.0 + g * (1.0 - sig))).astype(BF16)
        gu_ref[...] = (acc * g * sig).astype(BF16)

    return pl.pallas_call(
        body,
        grid=(hidden // tile,),
        in_specs=[
            const_spec((rows, width)),
            pl.BlockSpec((pieces, tile, part), lambda j: (0, j, 0)),
            pl.BlockSpec((rows, tile), lambda j: (0, j)),
            pl.BlockSpec((rows, tile), lambda j: (0, j)),
        ],
        out_specs=[pl.BlockSpec((rows, tile), lambda j: (0, j))] * 2,
        out_shape=[sds((rows, hidden), BF16)] * 2,
        cost_estimate=cost(2 * rows * width * hidden, 2 * width * hidden + 8 * rows * hidden, rows * hidden),
        name="hidden_back",
    )(grad_mlp, w_down, gate, up)


def mlp_back(grad_gate, grad_up, w_gate, w_up, tile):
    rows, hidden = grad_gate.shape
    width = w_gate.shape[0]

    def body(a_ref, b_ref, wa_ref, wb_ref, o_ref):
        o_ref[...] = dot(a_ref[...], wa_ref[...], NT) + dot(b_ref[...], wb_ref[...], NT)

    once = pl.Buffered(1)
    return pl.pallas_call(
        body,
        grid=(width // tile,),
        in_specs=[
            pl.BlockSpec((rows, hidden), lambda i: (0, 0), pipeline_mode=once),
            pl.BlockSpec((rows, hidden), lambda i: (0, 0), pipeline_mode=once),
            pl.BlockSpec((tile, hidden), lambda i: (i, 0)),
            pl.BlockSpec((tile, hidden), lambda i: (i, 0)),
        ],
        out_specs=pl.BlockSpec((rows, tile), lambda i: (0, i)),
        out_shape=sds((rows, width), F32),
        cost_estimate=cost(4 * rows * width * hidden, 4 * width * hidden + 4 * rows * hidden),
        name="mlp_back",
    )(grad_gate, grad_up, w_gate, w_up)


def middle_back(grad_normed, middle, cotangent, keep, gain, w_out, tile):
    rows, width = middle.shape
    depth = w_out.shape[0]

    def body(n_ref, m_ref, c_ref, k_ref, g_ref, w_ref, gm_ref, gb_ref, ga_ref, gg_ref):
        mid = m_ref[...]
        inv = lax.rsqrt(jnp.mean(mid * mid, -1, keepdims=True) + EPS)
        unit = mid * inv
        grad = n_ref[...]
        u = grad * g_ref[...]
        gmid = c_ref[...].astype(F32) + inv * (u - unit * jnp.mean(u * unit, -1, keepdims=True))
        branch = (k_ref[...] * gmid).astype(BF16)
        gm_ref[...] = gmid
        gb_ref[...] = branch
        ga_ref[...] = dot(branch, w_ref[...], NT).astype(BF16)
        total = jnp.sum(grad * unit, 0, keepdims=True)

        @pl.when(pl.program_id(0) == 0)
        def _():
            gg_ref[...] = total

        @pl.when(pl.program_id(0) > 0)
        def _():
            gg_ref[...] += total

    row = lambda i: (i, 0)
    return pl.pallas_call(
        body,
        grid=(rows // tile,),
        in_specs=[
            pl.BlockSpec((tile, width), row),
            pl.BlockSpec((tile, width), row),
            pl.BlockSpec((tile, width), row),
            pl.BlockSpec((tile, 1), row),
            const_spec((1, width)),
            const_spec((depth, width)),
        ],
        out_specs=[
            pl.BlockSpec((tile, width), row),
            pl.BlockSpec((tile, width), row),
            pl.BlockSpec((tile, depth), row),
            const_spec((1, width)),
        ],
        out_shape=[sds((rows, width), F32), sds((rows, width), BF16), sds((rows, depth), BF16), sds((1, width), F32)],
        cost_estimate=cost(2 * rows * depth * width, 2 * depth * width + 18 * rows * width),
        name="middle_back",
    )(grad_normed, middle, cotangent, keep, gain, w_out)


def input_back(grad_q, grad_kv, weights, x, grad_middle, gain, tile):
    rows, width = x.shape
    depth_q, depth_kv = grad_q.shape[1], grad_kv.shape[1]

    def body(q_ref, kv_ref, wq_ref, x_ref, m_ref, g_ref, o_ref, gg_ref):
        grad = dot(q_ref[...], wq_ref[:, :depth_q], NT) + dot(kv_ref[...], wq_ref[:, depth_q:], NT)
        xin = x_ref[...].astype(F32)
        inv = lax.rsqrt(jnp.mean(xin * xin, -1, keepdims=True) + EPS)
        unit = xin * inv
        u = grad * g_ref[...]
        o_ref[...] = (m_ref[...] + inv * (u - unit * jnp.mean(u * unit, -1, keepdims=True))).astype(BF16)
        total = jnp.sum(grad * unit, 0, keepdims=True)

        @pl.when(pl.program_id(0) == 0)
        def _():
            gg_ref[...] = total

        @pl.when(pl.program_id(0) > 0)
        def _():
            gg_ref[...] += total

    row = lambda i: (i, 0)
    return pl.pallas_call(
        body,
        grid=(rows // tile,),
        in_specs=[
            pl.BlockSpec((tile, depth_q), row),
            pl.BlockSpec((tile, depth_kv), row),
            pl.BlockSpec((width, depth_q + depth_kv), lambda i: (0, 0), pipeline_mode=pl.Buffered(1)),
            pl.BlockSpec((tile, width), row),
            pl.BlockSpec((tile, width), row),
            const_spec((1, width)),
        ],
        out_specs=[pl.BlockSpec((tile, width), row), const_spec((1, width))],
        out_shape=[sds((rows, width), BF16), sds((1, width), F32)],
        cost_estimate=cost(2 * rows * width * (depth_q + depth_kv), 2 * width * (depth_q + depth_kv) + 10 * rows * width),
        name="input_back",
    )(grad_q, grad_kv, weights, x, grad_middle, gain)


def weight_grad(side, chips, a_own, a_pair, b_own, b_pair, tile):
    rows, depth = a_own.shape
    width = b_own.shape[1]
    part = depth // (2 * len(chips))
    out_rows = depth // 2

    def body(side_ref, ao_ref, ap_ref, bo_ref, bp_ref, o_ref, to_ref, tp_ref):
        @pl.when(pl.program_id(0) == 0)
        def _():
            for k, chip in enumerate(chips):
                at = pl.ds(pl.multiple_of((2 * chip + side_ref[0]) * part, part), part)
                own = slice(k * part, (k + 1) * part)
                to_ref[own, :] = ao_ref[:, at].T
                tp_ref[own, :] = ap_ref[:, at].T

        o_ref[...] = (dot(to_ref[...], bo_ref[...]) + dot(tp_ref[...], bp_ref[...])).astype(BF16)

    return pl.pallas_call(
        body,
        grid_spec=pltpu.PrefetchScalarGridSpec(
            num_scalar_prefetch=1,
            grid=(width // tile,),
            in_specs=[
                pl.BlockSpec((rows, depth), lambda j, _: (0, 0), pipeline_mode=pl.Buffered(1)),
                pl.BlockSpec((rows, depth), lambda j, _: (0, 0), pipeline_mode=pl.Buffered(1)),
                pl.BlockSpec((rows, tile), lambda j, _: (0, j)),
                pl.BlockSpec((rows, tile), lambda j, _: (0, j)),
            ],
            out_specs=pl.BlockSpec((out_rows, tile), lambda j, _: (0, j)),
            scratch_shapes=[pltpu.VMEM((out_rows, rows), BF16)] * 2,
        ),
        out_shape=sds((out_rows, width), BF16),
        cost_estimate=cost(4 * rows * out_rows * width, 2 * out_rows * width + 4 * rows * width + 4 * rows * depth),
        name="weight_grad",
    )(side, a_own, a_pair, b_own, b_pair)


def on_device(
    layer_input,
    cotangent,
    positions,
    block_ids,
    skip_mask,
    attn_gain,
    w_query,
    w_key,
    w_value,
    w_out,
    mlp_gain,
    w_gate,
    w_up,
    w_down,
):
    seqs, local, width = layer_input.shape
    rows = seqs * local
    fsdp = lax.axis_size("fsdp")
    parts = lax.axis_size("ulysses")
    place = lax.axis_index("ulysses")
    side = lax.rem(lax.axis_index("fsdp"), 2).astype(jnp.int32).reshape(1)
    chips = fsdp // 2
    ring = [0, 1, 3, 2] if chips == 4 else list(range(chips))
    groups = [[2 * chip + core for chip in ring] for core in range(2)]
    pairs = [(i, i ^ 1) for i in range(fsdp)]
    ahead = min(parts - 1, -(-(BLOCK - 1) // local))
    query_width, pair_width = H * HD, KVH * HD
    tile = 512

    def after(v, *others):
        return lax.optimization_barrier((v,) + others)[0]

    def gather(v, tiled=True):
        return lax.all_gather(v, "fsdp", axis=0, tiled=tiled)

    def swap(v):
        return lax.ppermute(v, "fsdp", pairs)

    def scatter(v):
        return lax.psum_scatter(
            v, "fsdp", scatter_dimension=0, tiled=True, axis_index_groups=groups
        )

    def finish(v):
        middle = parts // 2
        if parts % 2:
            return lax.psum(v, "ulysses")

        def add(a, b):
            return (a.astype(F32) + b.astype(F32)).astype(BF16)

        for d in range(middle - 1):
            v = add(v, lax.ppermute(v, "ulysses", [(d, d + 1), (parts - 1 - d, parts - 2 - d)]))
        v = add(v, lax.ppermute(v, "ulysses", [(middle - 1, middle), (middle, middle - 1)]))
        for d in range(middle - 1, 0, -1):
            came = lax.ppermute(v, "ulysses", [(d, d - 1), (parts - 1 - d, parts - d)])
            v = jnp.where((place == d - 1) | (place == parts - d), came, v)
        return v

    def finish_in(v, pieces):
        step = v.shape[0] // pieces
        return jnp.concatenate([finish(v[i * step : (i + 1) * step]) for i in range(pieces)], 0)

    def grad_of(a, a_pair, b, b_pair):
        return weight_grad(side, ring, a, a_pair, b, b_pair, tile)

    def spread(v):
        ups, held = [], v
        for r in range(1, parts):
            held = lax.ppermute(held, "ulysses", [(i, i + 1) for i in range(r - 1, parts - 1)])
            ups.append(held)
        slots = [v] + ups
        for i in range(1, ahead + 1):
            down = lax.ppermute(v, "ulysses", [(z + i, z) for z in range(parts - i)])
            slots[parts - i] = jnp.where(place >= parts - i, slots[parts - i], down)
        return slots

    def collect(slots):
        total = slots[0].astype(F32)
        for i in range(1, ahead + 1):
            up = lax.ppermute(slots[parts - i], "ulysses", [(z, z + i) for z in range(parts - i)])
            total = total + up.astype(F32)
        held = slots[parts - 1]
        for r in range(parts - 1, 0, -1):
            came = lax.ppermute(held, "ulysses", [(i, i - 1) for i in range(r, parts)])
            if r > 1:
                held = (slots[r - 1].astype(F32) + came.astype(F32)).astype(BF16)
            else:
                total = total + came.astype(F32)
        return total

    gains = lax.all_gather(jnp.stack([attn_gain, mlp_gain]), "fsdp", axis=1, tiled=True).astype(F32)
    gain_one, gain_two = gains[0:1], gains[1:2]
    qkv_full = gather(jnp.concatenate([w_query, w_key, w_value], 1))
    out_full = gather(after(w_out, qkv_full))

    x = layer_input.reshape(rows, width)
    xf = x.astype(F32)
    inv_one = lax.rsqrt(jnp.mean(xf * xf, -1, keepdims=True) + EPS)
    normed_one = (xf * inv_one * gain_one).astype(BF16)
    keep = jnp.repeat((1 - skip_mask).astype(F32), local)[:, None]
    cot = cotangent.reshape(rows, width)
    grad_mlp = (keep * cot.astype(F32)).astype(BF16)

    half = HD // 2
    frequency = jnp.exp(jnp.arange(half, dtype=F32) * (-2.0 * math.log(10000.0) / HD))
    angles = positions.reshape(rows, 1).astype(F32) * frequency
    cosine = jnp.concatenate([jnp.cos(angles)] * 2, -1)
    sine = jnp.sin(angles)
    sine = jnp.concatenate([-sine, sine], -1)
    by_part = block_ids.reshape(seqs, parts, local)
    block_mine = lax.dynamic_slice_in_dim(by_part, place, 1, 1)
    order = lax.rem(place - jnp.arange(parts) + parts, parts)
    block_keys = jnp.take(by_part, order, 1).reshape(seqs, parts * local, 1)

    query, kv = project(normed_one, qkv_full, cosine, sine)
    slots = spread(kv)
    gate_full = gather(after(w_gate, out_full, slots[1]))
    one_pair, mlp_pair = swap(normed_one), swap(grad_mlp)
    attended, lse = attend(query, slots, block_keys, block_mine, seqs)
    middle, normed_two = out_project(attended, out_full, x, keep, gain_two, local)
    up_full = gather(after(w_up, gate_full, normed_two))
    gate = gate_matmul(normed_two, gate_full, tile)
    down_full = gather(after(w_down, up_full, gate), False)
    two_pair, att_pair = swap(normed_two), swap(attended)
    up, hidden = up_matmul(normed_two, up_full, gate, tile)

    hidden_pair = swap(hidden)
    down_part = grad_of(grad_mlp, mlp_pair, hidden, hidden_pair)
    down_sum = scatter(down_part)
    grad_gate, grad_up = hidden_back(after(grad_mlp, down_part), down_full, gate, up, tile)
    gate_pair, up_pair = swap(grad_gate), swap(grad_up)
    grad_normed_two = mlp_back(grad_gate, grad_up, gate_full, up_full, 256)
    gate_part = grad_of(normed_two, two_pair, after(grad_gate, grad_normed_two), gate_pair)
    gate_sum = scatter(after(gate_part, down_sum))
    grad_middle, grad_branch, grad_attended, grad_gain_two = middle_back(
        after(grad_normed_two, gate_part), middle, cot, keep, gain_two, out_full, local
    )
    branch_pair = swap(grad_branch)
    grad_query, *grad_slots = attend_back(
        query, slots, block_keys, block_mine, lse, grad_attended, cosine, sine, seqs
    )
    query_pair = swap(grad_query)
    up_part = grad_of(normed_two, two_pair, after(grad_up, grad_query), up_pair)
    up_sum = scatter(after(up_part, gate_sum))
    out_part = grad_of(attended, att_pair, after(grad_branch, up_part), branch_pair)
    out_sum = scatter(after(out_part, up_sum))
    query_part = grad_of(normed_one, one_pair, after(grad_query, out_part), query_pair)
    query_sum = scatter(after(query_part, out_sum))
    output = down_matmul(after(hidden, query_part), down_full, middle, keep)

    grad_kv = collect(grad_slots)
    grad_key = grad_kv[:, :pair_width].reshape(rows, KVH, HD)
    turned = grad_key * sine[:, None, :]
    turned = jnp.concatenate([turned[..., half:], turned[..., :half]], -1)
    grad_key = (grad_key * cosine[:, None, :] + turned).reshape(rows, pair_width)
    grad_kv = jnp.concatenate([grad_key, grad_kv[:, pair_width:]], 1).astype(BF16)
    kv_pair = swap(grad_kv)
    kv_part = grad_of(normed_one, one_pair, grad_kv, kv_pair)
    kv_sum = scatter(after(kv_part, query_sum))
    grad_input, grad_gain_one = input_back(
        grad_query, after(grad_kv, kv_part), qkv_full, x, grad_middle, gain_one, local
    )

    gain_sums = lax.psum(jnp.concatenate([grad_gain_one, grad_gain_two], 0), ("fsdp", "ulysses"))
    own = width // fsdp
    gain_shard = lax.dynamic_slice_in_dim(gain_sums, lax.axis_index("fsdp") * own, own, 1)
    out_down, out_gate, out_up, out_out, out_query, out_kv = (
        finish_in(v, pieces).astype(F32)
        for v, pieces in (
            (down_sum, 2),
            (gate_sum, 2),
            (up_sum, 2),
            (out_sum, 1),
            (query_sum, 1),
            (kv_sum, 1),
        )
    )
    return (
        output.reshape(layer_input.shape),
        grad_input.reshape(layer_input.shape),
        gain_shard[0],
        out_query,
        out_kv[:, :pair_width],
        out_kv[:, pair_width:],
        out_out,
        gain_shard[1],
        out_gate,
        out_up,
        out_down.T,
    )


def solution(mesh):
    return jax.shard_map(
        on_device,
        mesh=mesh,
        in_specs=(
            P("fsdp", "ulysses", None),
            P("fsdp", "ulysses", None),
            P("fsdp", "ulysses"),
            P("fsdp", None),
            P("fsdp"),
            P("fsdp"),
            P("fsdp", None),
            P("fsdp", None),
            P("fsdp", None),
            P("fsdp", None),
            P("fsdp"),
            P("fsdp", None),
            P("fsdp", None),
            P(None, "fsdp"),
        ),
        out_specs=(
            P("fsdp", "ulysses", None),
            P("fsdp", "ulysses", None),
            P("fsdp"),
            P("fsdp", None),
            P("fsdp", None),
            P("fsdp", None),
            P("fsdp", None),
            P("fsdp"),
            P("fsdp", None),
            P("fsdp", None),
            P(None, "fsdp"),
        ),
        check_vma=False,
    )
```

```python
import math

import jax
import jax.numpy as jnp
from jax import lax
from jax.experimental import pallas as pl
from jax.experimental.pallas import tpu as pltpu
from jax.sharding import PartitionSpec as P

H = 16
KVH = 4
HD = 128
GROUP = H // KVH
BLOCK = 256
EPS = 1e-05
F32 = jnp.float32
BF16 = jnp.bfloat16
LOG2E = math.log2(math.e)

NT = (((1,), (1,)), ((), ()))
NN = (((1,), (0,)), ((), ()))


def dot(a, b, dims=NN):
    return lax.dot_general(a, b, dims, preferred_element_type=F32)


def cost(flops, nbytes, trans=0):
    return pl.CostEstimate(flops=int(flops), bytes_accessed=int(nbytes), transcendentals=int(trans))


def const_spec(shape):
    zeros = (0,) * len(shape)
    return pl.BlockSpec(shape, lambda *_: zeros)


def sds(shape, dtype):
    return jax.ShapeDtypeStruct(shape, dtype)


def project(normed, weights, start, cosine, sine):
    rows, width = normed.shape
    tile = KVH * HD
    steps = (weights.shape[1] - start) // tile
    q_steps = H * HD // tile

    def body(x_ref, w_ref, c_ref, s_ref, q_ref, kv_ref):
        j = pl.program_id(0)
        y = dot(x_ref[...], w_ref[...])

        def turned():
            c, s = c_ref[...], s_ref[...]
            parts = []
            for h in range(KVH):
                v = y[:, h * HD : (h + 1) * HD]
                parts.append(v * c + pltpu.roll(v, HD // 2, 1) * s)
            return jnp.concatenate(parts, 1).astype(BF16)

        @pl.when(j < q_steps)
        def _():
            q_ref[...] = turned()

        @pl.when(j == q_steps)
        def _():
            kv_ref[...] = turned()

        @pl.when(j > q_steps)
        def _():
            kv_ref[...] = y.astype(BF16)

    return pl.pallas_call(
        body,
        grid=(steps,),
        in_specs=[
            const_spec((rows, width)),
            pl.BlockSpec((width, tile), lambda j: (0, start // tile + j)),
            const_spec((rows, HD)),
            const_spec((rows, HD)),
        ],
        out_specs=[
            pl.BlockSpec((rows, tile), lambda j: (0, jnp.minimum(j, q_steps - 1))),
            pl.BlockSpec((rows, tile), lambda j: (0, jnp.maximum(j - q_steps, 0))),
        ],
        out_shape=[sds((rows, H * HD), BF16), sds((rows, 2 * KVH * HD), BF16)],
        cost_estimate=cost(2 * rows * width * steps * tile, 2 * (width * steps * tile + 2 * rows * width)),
        name="project",
    )(normed, weights, cosine, sine)


def slot_specs(count, local, shift):
    return [pl.BlockSpec((local, HD), lambda s, j: (s, shift + j)) for _ in range(count)]


def attend(q, slots, block_keys, block_mine, seqs):
    rows = q.shape[0]
    local = rows // seqs
    parts = len(slots)
    full = parts * local
    scale = LOG2E / math.sqrt(HD)

    def body(q_ref, *refs):
        k_refs, v_refs = refs[:parts], refs[parts : 2 * parts]
        kid_ref, qid_ref, o_ref, lse_ref, bias_ref = refs[2 * parts :]

        @pl.when(pl.program_id(1) == 0)
        def _():
            bias_ref[...] = jnp.where(kid_ref[0] <= qid_ref[0], 0.0, -1e30)

        keys = jnp.concatenate([r[...] for r in k_refs], 0)
        values_t = jnp.concatenate([r[...] for r in v_refs], 0).T
        for h in range(GROUP):
            qh = q_ref[:, h * HD : (h + 1) * HD]
            s = dot(keys, qh, NT) * scale + bias_ref[...]
            top = jnp.max(s, 0, keepdims=True)
            e = jnp.exp2(s - top)
            total = jnp.sum(e, 0, keepdims=True)
            out_t = dot(values_t, e.astype(BF16)) * (1.0 / total)
            o_ref[:, h * HD : (h + 1) * HD] = out_t.T.astype(BF16)
            lse_ref[0, 0, h : h + 1, :] = top + jnp.log2(total)

    return pl.pallas_call(
        body,
        grid=(seqs, KVH),
        in_specs=[pl.BlockSpec((local, GROUP * HD), lambda s, j: (s, j))]
        + slot_specs(parts, local, 0)
        + slot_specs(parts, local, KVH)
        + [
            pl.BlockSpec((1, full, 1), lambda s, j: (s, 0, 0)),
            pl.BlockSpec((1, 1, local), lambda s, j: (s, 0, 0)),
        ],
        out_specs=[
            pl.BlockSpec((local, GROUP * HD), lambda s, j: (s, j)),
            pl.BlockSpec((1, 1, GROUP, local), lambda s, j: (s, j, 0, 0)),
        ],
        out_shape=[sds((rows, H * HD), BF16), sds((seqs, KVH, GROUP, local), F32)],
        scratch_shapes=[pltpu.VMEM((full, local), F32)],
        cost_estimate=cost(8 * rows * full * H * HD, 4 * rows * H * HD, rows * full * H),
        name="attend",
    )(q, *slots, *slots, block_keys, block_mine)


def attend_back(q, slots, block_keys, block_mine, lse, grad, cosine, sine, seqs):
    rows = q.shape[0]
    local = rows // seqs
    parts = len(slots)
    full = parts * local
    head_scale = 1.0 / math.sqrt(HD)
    scale = LOG2E * head_scale

    def body(q_ref, *refs):
        k_refs, v_refs = refs[:parts], refs[parts : 2 * parts]
        kid_ref, qid_ref, lse_ref, g_ref, c_ref, s_ref, dq_ref = refs[2 * parts : 2 * parts + 7]
        dkv_refs, bias_ref = refs[2 * parts + 7 : -1], refs[-1]
        j = pl.program_id(1)

        @pl.when(j == 0)
        def _():
            bias_ref[...] = jnp.where(kid_ref[0] <= qid_ref[0], 0.0, -1e30)

        keys = jnp.concatenate([r[...] for r in k_refs], 0)
        values = jnp.concatenate([r[...] for r in v_refs], 0)
        keys_t = keys.T
        c, sn = c_ref[...], s_ref[...]
        dk = jnp.zeros((full, HD), F32)
        dv = jnp.zeros((full, HD), F32)
        for h in range(GROUP):
            cols = slice(h * HD, (h + 1) * HD)
            qh = q_ref[:, cols]
            gh = g_ref[:, cols]
            p = jnp.exp2(dot(keys, qh, NT) * scale + bias_ref[...] - lse_ref[0, 0, h : h + 1, :])
            dp = dot(values, gh, NT)
            center = jnp.sum(p * dp, 0, keepdims=True)
            ds = (p * (dp - center)).astype(BF16)
            dv = dv + dot(p.astype(BF16), gh)
            dk = dk + dot(ds, qh)
            dq = dot(keys_t, ds).T * head_scale
            dq_ref[:, cols] = (dq * c + pltpu.roll(dq * sn, HD // 2, 1)).astype(BF16)
        k_at = pl.ds(pl.multiple_of(j * HD, HD), HD)
        v_at = pl.ds(pl.multiple_of((KVH + j) * HD, HD), HD)
        for part, ref in enumerate(dkv_refs):
            own = slice(part * local, (part + 1) * local)
            ref[:, k_at] = (dk[own] * head_scale).astype(BF16)
            ref[:, v_at] = dv[own].astype(BF16)

    row = lambda s, j: (s, 0)
    return pl.pallas_call(
        body,
        grid=(seqs, KVH),
        in_specs=[pl.BlockSpec((local, GROUP * HD), lambda s, j: (s, j))]
        + slot_specs(parts, local, 0)
        + slot_specs(parts, local, KVH)
        + [
            pl.BlockSpec((1, full, 1), lambda s, j: (s, 0, 0)),
            pl.BlockSpec((1, 1, local), lambda s, j: (s, 0, 0)),
            pl.BlockSpec((1, 1, GROUP, local), lambda s, j: (s, j, 0, 0)),
            pl.BlockSpec((local, GROUP * HD), lambda s, j: (s, j)),
            pl.BlockSpec((local, HD), row),
            pl.BlockSpec((local, HD), row),
        ],
        out_specs=[pl.BlockSpec((local, GROUP * HD), lambda s, j: (s, j))]
        + [pl.BlockSpec((local, 2 * KVH * HD), row)] * parts,
        out_shape=[sds((rows, H * HD), BF16)] + [sds((rows, 2 * KVH * HD), BF16)] * parts,
        scratch_shapes=[pltpu.VMEM((full, local), F32)],
        cost_estimate=cost(20 * rows * full * H * HD, 8 * rows * H * HD, rows * full * H),
        name="attend_back",
    )(q, *slots, *slots, block_keys, block_mine, lse, grad, cosine, sine)


def out_project(attended, w_out, x, keep, gain, tile):
    rows, width = x.shape
    depth = attended.shape[1]

    def body(a_ref, w_ref, x_ref, k_ref, g_ref, m_ref, n_ref):
        mid = x_ref[...].astype(F32) + k_ref[...] * dot(a_ref[...], w_ref[...])
        inv = lax.rsqrt(jnp.mean(mid * mid, -1, keepdims=True) + EPS)
        m_ref[...] = mid
        n_ref[...] = (mid * inv * g_ref[...]).astype(BF16)

    return pl.pallas_call(
        body,
        grid=(rows // tile,),
        in_specs=[
            pl.BlockSpec((tile, depth), lambda i: (i, 0)),
            const_spec((depth, width)),
            pl.BlockSpec((tile, width), lambda i: (i, 0)),
            pl.BlockSpec((tile, 1), lambda i: (i, 0)),
            const_spec((1, width)),
        ],
        out_specs=[pl.BlockSpec((tile, width), lambda i: (i, 0))] * 2,
        out_shape=[sds((rows, width), F32), sds((rows, width), BF16)],
        cost_estimate=cost(2 * rows * depth * width, 2 * depth * width + 10 * rows * width),
        name="out_project",
    )(attended, w_out, x, keep, gain)


def gate_matmul(normed, w_gate, hidden, tile):
    rows, width = normed.shape

    def body(x_ref, w_ref, g_ref):
        g_ref[...] = dot(x_ref[...], w_ref[...]).astype(BF16)

    return pl.pallas_call(
        body,
        grid=(hidden // tile,),
        in_specs=[const_spec((rows, width)), pl.BlockSpec((width, tile), lambda j: (0, j))],
        out_specs=pl.BlockSpec((rows, tile), lambda j: (0, j)),
        out_shape=sds((rows, hidden), BF16),
        cost_estimate=cost(2 * rows * width * hidden, 2 * width * hidden + 2 * rows * hidden),
        name="gate_matmul",
    )(normed, w_gate)


def up_matmul(normed, w_up, start, gate, tile):
    rows, width = normed.shape
    hidden = gate.shape[1]

    def body(x_ref, w_ref, g_ref, u_ref, h_ref):
        up = dot(x_ref[...], w_ref[...])
        g = g_ref[...].astype(F32)
        u_ref[...] = up.astype(BF16)
        h_ref[...] = (g * jax.nn.sigmoid(g) * up).astype(BF16)

    return pl.pallas_call(
        body,
        grid=(hidden // tile,),
        in_specs=[
            const_spec((rows, width)),
            pl.BlockSpec((width, tile), lambda j: (0, start // tile + j)),
            pl.BlockSpec((rows, tile), lambda j: (0, j)),
        ],
        out_specs=[pl.BlockSpec((rows, tile), lambda j: (0, j))] * 2,
        out_shape=[sds((rows, hidden), BF16)] * 2,
        cost_estimate=cost(2 * rows * width * hidden, 2 * width * hidden + 6 * rows * hidden, rows * hidden),
        name="up_matmul",
    )(normed, w_up, gate)


def down_matmul(hidden, w_down, middle, keep):
    rows, depth = hidden.shape
    pieces, _, tile = w_down.shape

    def body(h_ref, w_ref, m_ref, k_ref, o_ref):
        o_ref[...] = (m_ref[...] + k_ref[...] * dot(h_ref[...], w_ref[0])).astype(BF16)

    return pl.pallas_call(
        body,
        grid=(pieces,),
        in_specs=[
            const_spec((rows, depth)),
            pl.BlockSpec((1, depth, tile), lambda i: (i, 0, 0)),
            pl.BlockSpec((rows, tile), lambda i: (0, i)),
            const_spec((rows, 1)),
        ],
        out_specs=pl.BlockSpec((rows, tile), lambda i: (0, i)),
        out_shape=sds((rows, pieces * tile), BF16),
        cost_estimate=cost(2 * rows * depth * pieces * tile, 2 * depth * pieces * tile + 2 * rows * depth),
        name="down_matmul",
    )(hidden, w_down, middle, keep)


def hidden_back(grad_mlp, w_down, gate, up, tile):
    rows, width = grad_mlp.shape
    pieces, hidden, part = w_down.shape

    def body(m_ref, w_ref, g_ref, u_ref, gg_ref, gu_ref):
        acc = dot(m_ref[:, :part], w_ref[0], NT)
        for i in range(1, pieces):
            acc = acc + dot(m_ref[:, i * part : (i + 1) * part], w_ref[i], NT)
        g = g_ref[...].astype(F32)
        u = u_ref[...].astype(F32)
        sig = jax.nn.sigmoid(g)
        gg_ref[...] = (acc * u * sig * (1.0 + g * (1.0 - sig))).astype(BF16)
        gu_ref[...] = (acc * g * sig).astype(BF16)

    return pl.pallas_call(
        body,
        grid=(hidden // tile,),
        in_specs=[
            const_spec((rows, width)),
            pl.BlockSpec((pieces, tile, part), lambda j: (0, j, 0)),
            pl.BlockSpec((rows, tile), lambda j: (0, j)),
            pl.BlockSpec((rows, tile), lambda j: (0, j)),
        ],
        out_specs=[pl.BlockSpec((rows, tile), lambda j: (0, j))] * 2,
        out_shape=[sds((rows, hidden), BF16)] * 2,
        cost_estimate=cost(2 * rows * width * hidden, 2 * width * hidden + 8 * rows * hidden, rows * hidden),
        name="hidden_back",
    )(grad_mlp, w_down, gate, up)


def mlp_back(grad_gate, grad_up, weights, tile):
    rows, hidden = grad_gate.shape
    width = weights.shape[0]

    def body(a_ref, b_ref, wa_ref, wb_ref, o_ref):
        o_ref[...] = dot(a_ref[...], wa_ref[...], NT) + dot(b_ref[...], wb_ref[...], NT)

    once = pl.Buffered(1)
    return pl.pallas_call(
        body,
        grid=(width // tile,),
        in_specs=[
            pl.BlockSpec((rows, hidden), lambda i: (0, 0), pipeline_mode=once),
            pl.BlockSpec((rows, hidden), lambda i: (0, 0), pipeline_mode=once),
            pl.BlockSpec((tile, hidden), lambda i: (i, 0)),
            pl.BlockSpec((tile, hidden), lambda i: (i, 1)),
        ],
        out_specs=pl.BlockSpec((rows, tile), lambda i: (0, i)),
        out_shape=sds((rows, width), F32),
        cost_estimate=cost(4 * rows * width * hidden, 4 * width * hidden + 4 * rows * hidden),
        name="mlp_back",
    )(grad_gate, grad_up, weights, weights)


def middle_back(grad_normed, middle, cotangent, keep, gain, w_out, tile):
    rows, width = middle.shape
    depth = w_out.shape[0]

    def body(n_ref, m_ref, c_ref, k_ref, g_ref, w_ref, gm_ref, gb_ref, ga_ref, gg_ref):
        mid = m_ref[...]
        inv = lax.rsqrt(jnp.mean(mid * mid, -1, keepdims=True) + EPS)
        unit = mid * inv
        grad = n_ref[...]
        u = grad * g_ref[...]
        gmid = c_ref[...].astype(F32) + inv * (u - unit * jnp.mean(u * unit, -1, keepdims=True))
        branch = (k_ref[...] * gmid).astype(BF16)
        gm_ref[...] = gmid
        gb_ref[...] = branch
        ga_ref[...] = dot(branch, w_ref[...], NT).astype(BF16)
        total = jnp.sum(grad * unit, 0, keepdims=True)

        @pl.when(pl.program_id(0) == 0)
        def _():
            gg_ref[...] = total

        @pl.when(pl.program_id(0) > 0)
        def _():
            gg_ref[...] += total

    row = lambda i: (i, 0)
    return pl.pallas_call(
        body,
        grid=(rows // tile,),
        in_specs=[
            pl.BlockSpec((tile, width), row),
            pl.BlockSpec((tile, width), row),
            pl.BlockSpec((tile, width), row),
            pl.BlockSpec((tile, 1), row),
            const_spec((1, width)),
            const_spec((depth, width)),
        ],
        out_specs=[
            pl.BlockSpec((tile, width), row),
            pl.BlockSpec((tile, width), row),
            pl.BlockSpec((tile, depth), row),
            const_spec((1, width)),
        ],
        out_shape=[sds((rows, width), F32), sds((rows, width), BF16), sds((rows, depth), BF16), sds((1, width), F32)],
        cost_estimate=cost(2 * rows * depth * width, 2 * depth * width + 18 * rows * width),
        name="middle_back",
    )(grad_normed, middle, cotangent, keep, gain, w_out)


def input_back(grad_q, grad_kv, weights, start, x, grad_middle, gain, tile):
    rows, width = x.shape
    depth_q, depth_kv = grad_q.shape[1], grad_kv.shape[1]

    def body(q_ref, kv_ref, wq_ref, wkv_ref, x_ref, m_ref, g_ref, o_ref, gg_ref):
        grad = dot(q_ref[...], wq_ref[...], NT) + dot(kv_ref[...], wkv_ref[...], NT)
        xin = x_ref[...].astype(F32)
        inv = lax.rsqrt(jnp.mean(xin * xin, -1, keepdims=True) + EPS)
        unit = xin * inv
        u = grad * g_ref[...]
        o_ref[...] = (m_ref[...] + inv * (u - unit * jnp.mean(u * unit, -1, keepdims=True))).astype(BF16)
        total = jnp.sum(grad * unit, 0, keepdims=True)

        @pl.when(pl.program_id(0) == 0)
        def _():
            gg_ref[...] = total

        @pl.when(pl.program_id(0) > 0)
        def _():
            gg_ref[...] += total

    row = lambda i: (i, 0)
    return pl.pallas_call(
        body,
        grid=(rows // tile,),
        in_specs=[
            pl.BlockSpec((tile, depth_q), row),
            pl.BlockSpec((tile, depth_kv), row),
            pl.BlockSpec((width, depth_q), lambda i: (0, start // depth_q), pipeline_mode=pl.Buffered(1)),
            pl.BlockSpec(
                (width, depth_kv), lambda i: (0, (start + depth_q) // depth_kv), pipeline_mode=pl.Buffered(1)
            ),
            pl.BlockSpec((tile, width), row),
            pl.BlockSpec((tile, width), row),
            const_spec((1, width)),
        ],
        out_specs=[pl.BlockSpec((tile, width), row), const_spec((1, width))],
        out_shape=[sds((rows, width), BF16), sds((1, width), F32)],
        cost_estimate=cost(2 * rows * width * (depth_q + depth_kv), 2 * width * (depth_q + depth_kv) + 10 * rows * width),
        name="input_back",
    )(grad_q, grad_kv, weights, weights, x, grad_middle, gain)


def weight_grad(side, chips, a_own, a_pair, b_own, b_pair, tile, total=None, first=0, into=None):
    rows, depth = a_own.shape
    width = b_own.shape[1]
    part = depth // (2 * len(chips))
    out_rows = depth // 2
    held = [] if into is None else [into]

    def body(side_ref, ao_ref, ap_ref, bo_ref, bp_ref, *refs):
        o_ref, to_ref, tp_ref = refs[len(held) :]

        @pl.when(pl.program_id(0) == 0)
        def _():
            for k, chip in enumerate(chips):
                at = pl.ds(pl.multiple_of((2 * chip + side_ref[0]) * part, part), part)
                own = slice(k * part, (k + 1) * part)
                to_ref[own, :] = ao_ref[:, at].T
                tp_ref[own, :] = ap_ref[:, at].T

        o_ref[...] = (dot(to_ref[...], bo_ref[...]) + dot(tp_ref[...], bp_ref[...])).astype(BF16)

    return pl.pallas_call(
        body,
        grid_spec=pltpu.PrefetchScalarGridSpec(
            num_scalar_prefetch=1,
            grid=(width // tile,),
            in_specs=[
                pl.BlockSpec((rows, depth), lambda j, _: (0, 0), pipeline_mode=pl.Buffered(1)),
                pl.BlockSpec((rows, depth), lambda j, _: (0, 0), pipeline_mode=pl.Buffered(1)),
                pl.BlockSpec((rows, tile), lambda j, _: (0, j)),
                pl.BlockSpec((rows, tile), lambda j, _: (0, j)),
            ]
            + [pl.BlockSpec(memory_space=pl.ANY)] * len(held),
            out_specs=pl.BlockSpec((out_rows, tile), lambda j, _: (0, first + j)),
            scratch_shapes=[pltpu.VMEM((out_rows, rows), BF16)] * 2,
        ),
        out_shape=sds((out_rows, width if total is None else total), BF16),
        input_output_aliases={5: 0} if held else {},
        cost_estimate=cost(4 * rows * out_rows * width, 2 * out_rows * width + 4 * rows * width + 4 * rows * depth),
        name="weight_grad",
    )(side, a_own, a_pair, b_own, b_pair, *held)


def on_device(
    layer_input,
    cotangent,
    positions,
    block_ids,
    skip_mask,
    attn_gain,
    w_query,
    w_key,
    w_value,
    w_out,
    mlp_gain,
    w_gate,
    w_up,
    w_down,
):
    seqs, local, width = layer_input.shape
    rows = seqs * local
    fsdp = lax.axis_size("fsdp")
    parts = lax.axis_size("ulysses")
    place = lax.axis_index("ulysses")
    side = lax.rem(lax.axis_index("fsdp"), 2).astype(jnp.int32).reshape(1)
    chips = fsdp // 2
    ring = [0, 1, 3, 2] if chips == 4 else list(range(chips))
    groups = [[2 * chip + core for chip in ring] for core in range(2)]
    pairs = [(i, i ^ 1) for i in range(fsdp)]
    ahead = min(parts - 1, -(-(BLOCK - 1) // local))
    query_width, pair_width = H * HD, KVH * HD
    hidden_width = w_gate.shape[1]
    tile = 512

    def after(v, *others):
        return lax.optimization_barrier((v,) + others)[0]

    def gather(v, tiled=True):
        return lax.all_gather(v, "fsdp", axis=0, tiled=tiled)

    def swap(v):
        return lax.ppermute(v, "fsdp", pairs)

    def scatter(v):
        return lax.psum_scatter(
            v, "fsdp", scatter_dimension=0, tiled=True, axis_index_groups=groups
        )

    def finish(v):
        return lax.psum(v, "ulysses")

    middle_part = parts // 2
    hops = [
        ([(d, d + 1), (parts - 1 - d, parts - 2 - d)], None) for d in range(middle_part - 1)
    ]
    hops.append(([(middle_part - 1, middle_part), (middle_part, middle_part - 1)], None))
    hops += [
        ([(d, d - 1), (parts - 1 - d, parts - d)], (place == d - 1) | (place == parts - d))
        for d in range(middle_part - 1, 0, -1)
    ]
    under_way = []

    def add(a, b):
        return (a.astype(F32) + b.astype(F32)).astype(BF16)

    def tick(new, *gates):
        for chunk in under_way:
            came, takes = chunk["came"], hops[chunk["hop"] - 1][1]
            chunk["v"] = add(chunk["v"], came) if takes is None else jnp.where(takes, came, chunk["v"])
        for out, k, v in new:
            under_way.append({"out": out, "k": k, "v": v, "hop": 0})
        held = lax.optimization_barrier(tuple(c["v"] for c in under_way) + gates)
        for chunk, v in zip(list(under_way), held):
            chunk["v"] = v
            if chunk["hop"] == len(hops):
                chunk["out"][chunk["k"]] = v
                under_way.remove(chunk)
            else:
                chunk["came"] = lax.ppermute(v, "ulysses", hops[chunk["hop"]][0])
                chunk["hop"] += 1
        return held[0]

    def chunks(v, count):
        out, step = {}, v.shape[0] // count
        return out, [(out, k, v[k * step : (k + 1) * step]) for k in range(count)]

    def joined(out):
        return jnp.concatenate([out[k] for k in range(len(out))], 0)

    def grad_of(*operands, **where):
        return weight_grad(side, ring, *operands, tile, **where)

    def spread(v):
        ups, held = [], v
        for r in range(1, parts):
            held = lax.ppermute(held, "ulysses", [(i, i + 1) for i in range(r - 1, parts - 1)])
            ups.append(held)
        slots = [v] + ups
        for i in range(1, ahead + 1):
            down = lax.ppermute(v, "ulysses", [(z + i, z) for z in range(parts - i)])
            slots[parts - i] = jnp.where(place >= parts - i, slots[parts - i], down)
        return slots

    def collect(slots):
        total = slots[0].astype(F32)
        ups = [
            lax.ppermute(slots[parts - i], "ulysses", [(z, z + i) for z in range(parts - i)])
            for i in range(1, ahead + 1)
        ]
        held = slots[parts - 1]
        for r in range(parts - 1, 0, -1):
            came = lax.ppermute(held, "ulysses", [(i, i - 1) for i in range(r, parts)])
            if r > 1:
                held = yield add(slots[r - 1], came)
            else:
                for up in ups:
                    total = total + up.astype(F32)
                yield total + came.astype(F32)

    gains = lax.all_gather(jnp.stack([attn_gain, mlp_gain]), "fsdp", axis=1, tiled=True).astype(F32)
    gain_one, gain_two = gains[0:1], gains[1:2]
    att_full = gather(jnp.concatenate([w_out, w_query, w_key, w_value], 1))
    mlp_full = gather(after(jnp.concatenate([w_gate, w_up], 1), att_full))

    first_sum = finish(w_key)
    x = layer_input.reshape(rows, width)
    xf = x.astype(F32)
    inv_one = lax.rsqrt(jnp.mean(xf * xf, -1, keepdims=True) + EPS)
    normed_one = (xf * inv_one * gain_one).astype(BF16)
    keep = jnp.repeat((1 - skip_mask).astype(F32), local)[:, None]
    cot = cotangent.reshape(rows, width)
    grad_mlp = (keep * cot.astype(F32)).astype(BF16)

    half = HD // 2
    frequency = jnp.exp(jnp.arange(half, dtype=F32) * (-2.0 * math.log(10000.0) / HD))
    angles = positions.reshape(rows, 1).astype(F32) * frequency
    cosine = jnp.concatenate([jnp.cos(angles)] * 2, -1)
    sine = jnp.sin(angles)
    sine = jnp.concatenate([-sine, sine], -1)
    by_part = block_ids.reshape(seqs, parts, local)
    block_mine = lax.dynamic_slice_in_dim(by_part, place, 1, 1)
    order = lax.rem(place - jnp.arange(parts) + parts, parts)
    block_keys = jnp.take(by_part, order, 1).reshape(seqs, parts * local, 1)

    query, kv = project(normed_one, att_full, width, cosine, sine)
    slots = spread(kv)
    one_pair, mlp_pair = swap(normed_one), swap(grad_mlp)
    attended, lse = attend(query, slots, block_keys, block_mine, seqs)
    middle, normed_two = out_project(attended, att_full, x, keep, gain_two, local)
    gate = gate_matmul(normed_two, mlp_full, hidden_width, tile)
    down_full = gather(after(w_down, mlp_full, normed_two), False)
    two_pair, att_pair = swap(normed_two), swap(attended)
    up, hidden = up_matmul(normed_two, mlp_full, hidden_width, gate, tile)

    hidden_pair = swap(hidden)
    down_part = grad_of(grad_mlp, mlp_pair, hidden, hidden_pair)
    down_sum = scatter(down_part)
    grad_gate, grad_up = hidden_back(after(grad_mlp, down_part), down_full, gate, up, tile)
    gate_pair, up_pair = swap(grad_gate), swap(grad_up)
    grad_normed_two = mlp_back(grad_gate, grad_up, mlp_full, 256)
    gate_part = grad_of(normed_two, two_pair, after(grad_gate, grad_normed_two), gate_pair)
    gate_sum = scatter(after(gate_part, down_sum))
    down_all = finish(after(down_sum, gate_part, first_sum))
    grad_middle, grad_branch, grad_attended, grad_gain_two = middle_back(
        after(grad_normed_two, gate_part), middle, cot, keep, gain_two, att_full, local
    )
    branch_pair = swap(grad_branch)
    grad_query, *grad_slots = attend_back(
        query, slots, block_keys, block_mine, lse, grad_attended, cosine, sine, seqs
    )
    query_pair = swap(grad_query)
    collecting = collect(grad_slots)
    kv_held = next(collecting)
    up_part = grad_of(normed_two, two_pair, after(grad_up, grad_query), up_pair)
    up_sum = scatter(after(up_part, gate_sum))
    columns = query_width + width
    att_part = grad_of(
        attended, att_pair, after(grad_branch, up_part, gate_sum), branch_pair, total=columns, first=query_width // tile
    )
    gate_all = finish(after(gate_sum, up_part, down_all))
    att_part = grad_of(
        normed_one, one_pair, after(grad_query, down_all, kv_held), query_pair, total=columns, into=att_part
    )
    for _ in range(parts - 3):
        kv_held = collecting.send(kv_held)
    att_sum = scatter(after(att_part, up_sum))
    up_all, fresh = chunks(up_sum, 2)
    token = tick(fresh[:1], att_part, kv_held, gate_all)
    grad_kv = collecting.send(after(kv_held, token))
    output = down_matmul(after(hidden, token), down_full, middle, keep)
    token = tick(fresh[1:], output)
    grad_kv = after(grad_kv, token)
    out_down = after(down_all, token).astype(F32).T
    grad_key = grad_kv[:, :pair_width].reshape(rows, KVH, HD)
    turned = grad_key * sine[:, None, :]
    turned = jnp.concatenate([turned[..., half:], turned[..., :half]], -1)
    grad_key = (grad_key * cosine[:, None, :] + turned).reshape(rows, pair_width)
    grad_kv = jnp.concatenate([grad_key, grad_kv[:, pair_width:]], 1).astype(BF16)
    kv_pair = swap(grad_kv)
    kv_part = grad_of(normed_one, one_pair, after(grad_kv, token), kv_pair)
    grad_input, grad_gain_one = input_back(
        grad_query, after(grad_kv, kv_part, out_down), att_full, width, x, grad_middle, gain_one, local
    )
    gain_grads = jnp.concatenate([grad_gain_one, grad_gain_two], 0)
    gain_grads = (gain_grads + swap(gain_grads)).reshape(2, chips, 2, width // fsdp)
    gain_grads = lax.dynamic_index_in_dim(gain_grads, side[0], 2, False)
    gain_grads = jnp.stack([gain_grads[:, chip] for chip in ring], 1).reshape(2, width // 2)
    gain_part = jnp.pad(gain_grads.T, ((0, 0), (0, HD - 2))).astype(BF16)
    kv_sum = scatter(after(jnp.concatenate([kv_part, gain_part], 1), att_sum))
    att_all, fresh = chunks(att_sum, 2)
    token = tick(fresh[:1], grad_input)
    out_gate = after(gate_all, token).astype(F32)
    token = tick(fresh[1:], out_gate)
    kv_sums, fresh = chunks(kv_sum, 1)
    token = tick(fresh)
    while under_way:
        token = tick([])
    out_up = joined(up_all).astype(F32)
    att_all, kv_sums = joined(att_all), joined(kv_sums)
    out_query = att_all[:, :query_width].astype(F32)
    out_out = att_all[:, query_width:].astype(F32)
    out_key = kv_sums[:, :pair_width].astype(F32)
    out_value = kv_sums[:, pair_width : 2 * pair_width].astype(F32)
    out_gains = kv_sums[:, 2 * pair_width : 2 * pair_width + 2].astype(F32).T + 0.0 * first_sum[0, 0].astype(F32)
    return (
        output.reshape(layer_input.shape),
        grad_input.reshape(layer_input.shape),
        out_gains[0],
        out_query,
        out_key,
        out_value,
        out_out,
        out_gains[1],
        out_gate,
        out_up,
        out_down,
    )


def solution(mesh):
    return jax.shard_map(
        on_device,
        mesh=mesh,
        in_specs=(
            P("fsdp", "ulysses", None),
            P("fsdp", "ulysses", None),
            P("fsdp", "ulysses"),
            P("fsdp", None),
            P("fsdp"),
            P("fsdp"),
            P("fsdp", None),
            P("fsdp", None),
            P("fsdp", None),
            P("fsdp", None),
            P("fsdp"),
            P("fsdp", None),
            P("fsdp", None),
            P(None, "fsdp"),
        ),
        out_specs=(
            P("fsdp", "ulysses", None),
            P("fsdp", "ulysses", None),
            P("fsdp"),
            P("fsdp", None),
            P("fsdp", None),
            P("fsdp", None),
            P("fsdp", None),
            P("fsdp"),
            P("fsdp", None),
            P("fsdp", None),
            P(None, "fsdp"),
        ),
        check_vma=False,
    )
```

```python
import math

import jax
import jax.numpy as jnp
from jax import lax
from jax.experimental import pallas as pl
from jax.experimental.pallas import tpu as pltpu
from jax.sharding import PartitionSpec as P

H = 16
KVH = 4
HD = 128
GROUP = H // KVH
BLOCK = 256
EPS = 1e-05
F32 = jnp.float32
BF16 = jnp.bfloat16
LOG2E = math.log2(math.e)

NT = (((1,), (1,)), ((), ()))
NN = (((1,), (0,)), ((), ()))


def dot(a, b, dims=NN):
    return lax.dot_general(a, b, dims, preferred_element_type=F32)


def cost(flops, nbytes, trans=0):
    return pl.CostEstimate(flops=int(flops), bytes_accessed=int(nbytes), transcendentals=int(trans))


def const_spec(shape):
    zeros = (0,) * len(shape)
    return pl.BlockSpec(shape, lambda *_: zeros)


def sds(shape, dtype):
    return jax.ShapeDtypeStruct(shape, dtype)


def project(normed, weights, start, cosine, sine):
    rows, width = normed.shape
    tile = KVH * HD
    steps = (weights.shape[1] - start) // tile
    q_steps = H * HD // tile

    def body(x_ref, w_ref, c_ref, s_ref, q_ref, kv_ref):
        j = pl.program_id(0)
        y = dot(x_ref[...], w_ref[...])

        def turned():
            c, s = c_ref[...], s_ref[...]
            parts = []
            for h in range(KVH):
                v = y[:, h * HD : (h + 1) * HD]
                parts.append(v * c + pltpu.roll(v, HD // 2, 1) * s)
            return jnp.concatenate(parts, 1).astype(BF16)

        @pl.when(j < q_steps)
        def _():
            q_ref[...] = turned()

        @pl.when(j == q_steps)
        def _():
            kv_ref[...] = turned()

        @pl.when(j > q_steps)
        def _():
            kv_ref[...] = y.astype(BF16)

    return pl.pallas_call(
        body,
        grid=(steps,),
        in_specs=[
            const_spec((rows, width)),
            pl.BlockSpec((width, tile), lambda j: (0, start // tile + j)),
            const_spec((rows, HD)),
            const_spec((rows, HD)),
        ],
        out_specs=[
            pl.BlockSpec((rows, tile), lambda j: (0, jnp.minimum(j, q_steps - 1))),
            pl.BlockSpec((rows, tile), lambda j: (0, jnp.maximum(j - q_steps, 0))),
        ],
        out_shape=[sds((rows, H * HD), BF16), sds((rows, 2 * KVH * HD), BF16)],
        cost_estimate=cost(2 * rows * width * steps * tile, 2 * (width * steps * tile + 2 * rows * width)),
        name="project",
    )(normed, weights, cosine, sine)


def slot_specs(count, local, shift):
    return [pl.BlockSpec((local, HD), lambda s, j: (s, shift + j)) for _ in range(count)]


def attend(q, slots, block_keys, block_mine, seqs):
    rows = q.shape[0]
    local = rows // seqs
    parts = len(slots)
    full = parts * local
    scale = LOG2E / math.sqrt(HD)

    def body(q_ref, *refs):
        k_refs, v_refs = refs[:parts], refs[parts : 2 * parts]
        kid_ref, qid_ref, o_ref, lse_ref, bias_ref = refs[2 * parts :]

        @pl.when(pl.program_id(1) == 0)
        def _():
            bias_ref[...] = jnp.where(kid_ref[0] <= qid_ref[0], 0.0, -1e30)

        keys = jnp.concatenate([r[...] for r in k_refs], 0)
        values_t = jnp.concatenate([r[...] for r in v_refs], 0).T
        for h in range(GROUP):
            qh = q_ref[:, h * HD : (h + 1) * HD]
            s = dot(keys, qh, NT) * scale + bias_ref[...]
            top = jnp.max(s, 0, keepdims=True)
            e = jnp.exp2(s - top)
            total = jnp.sum(e, 0, keepdims=True)
            out_t = dot(values_t, e.astype(BF16)) * (1.0 / total)
            o_ref[:, h * HD : (h + 1) * HD] = out_t.T.astype(BF16)
            lse_ref[0, 0, h : h + 1, :] = top + jnp.log2(total)

    return pl.pallas_call(
        body,
        grid=(seqs, KVH),
        in_specs=[pl.BlockSpec((local, GROUP * HD), lambda s, j: (s, j))]
        + slot_specs(parts, local, 0)
        + slot_specs(parts, local, KVH)
        + [
            pl.BlockSpec((1, full, 1), lambda s, j: (s, 0, 0)),
            pl.BlockSpec((1, 1, local), lambda s, j: (s, 0, 0)),
        ],
        out_specs=[
            pl.BlockSpec((local, GROUP * HD), lambda s, j: (s, j)),
            pl.BlockSpec((1, 1, GROUP, local), lambda s, j: (s, j, 0, 0)),
        ],
        out_shape=[sds((rows, H * HD), BF16), sds((seqs, KVH, GROUP, local), F32)],
        scratch_shapes=[pltpu.VMEM((full, local), F32)],
        cost_estimate=cost(8 * rows * full * H * HD, 4 * rows * H * HD, rows * full * H),
        name="attend",
    )(q, *slots, *slots, block_keys, block_mine)


def attend_back(q, slots, block_keys, block_mine, lse, grad, cosine, sine, seqs):
    rows = q.shape[0]
    local = rows // seqs
    parts = len(slots)
    full = parts * local
    head_scale = 1.0 / math.sqrt(HD)
    scale = LOG2E * head_scale

    def body(q_ref, *refs):
        k_refs, v_refs = refs[:parts], refs[parts : 2 * parts]
        kid_ref, qid_ref, lse_ref, g_ref, c_ref, s_ref, dq_ref = refs[2 * parts : 2 * parts + 7]
        dkv_refs, bias_ref = refs[2 * parts + 7 : -1], refs[-1]
        j = pl.program_id(1)

        @pl.when(j == 0)
        def _():
            bias_ref[...] = jnp.where(kid_ref[0] <= qid_ref[0], 0.0, -1e30)

        keys = jnp.concatenate([r[...] for r in k_refs], 0)
        values = jnp.concatenate([r[...] for r in v_refs], 0)
        keys_t = keys.T
        c, sn = c_ref[...], s_ref[...]
        dk = jnp.zeros((full, HD), F32)
        dv = jnp.zeros((full, HD), F32)
        for h in range(GROUP):
            cols = slice(h * HD, (h + 1) * HD)
            qh = q_ref[:, cols]
            gh = g_ref[:, cols]
            p = jnp.exp2(dot(keys, qh, NT) * scale + bias_ref[...] - lse_ref[0, 0, h : h + 1, :])
            dp = dot(values, gh, NT)
            center = jnp.sum(p * dp, 0, keepdims=True)
            ds = (p * (dp - center)).astype(BF16)
            dv = dv + dot(p.astype(BF16), gh)
            dk = dk + dot(ds, qh)
            dq = dot(keys_t, ds).T * head_scale
            dq_ref[:, cols] = (dq * c + pltpu.roll(dq * sn, HD // 2, 1)).astype(BF16)
        k_at = pl.ds(pl.multiple_of(j * HD, HD), HD)
        v_at = pl.ds(pl.multiple_of((KVH + j) * HD, HD), HD)
        for part, ref in enumerate(dkv_refs):
            own = slice(part * local, (part + 1) * local)
            ref[:, k_at] = (dk[own] * head_scale).astype(BF16)
            ref[:, v_at] = dv[own].astype(BF16)

    row = lambda s, j: (s, 0)
    return pl.pallas_call(
        body,
        grid=(seqs, KVH),
        in_specs=[pl.BlockSpec((local, GROUP * HD), lambda s, j: (s, j))]
        + slot_specs(parts, local, 0)
        + slot_specs(parts, local, KVH)
        + [
            pl.BlockSpec((1, full, 1), lambda s, j: (s, 0, 0)),
            pl.BlockSpec((1, 1, local), lambda s, j: (s, 0, 0)),
            pl.BlockSpec((1, 1, GROUP, local), lambda s, j: (s, j, 0, 0)),
            pl.BlockSpec((local, GROUP * HD), lambda s, j: (s, j)),
            pl.BlockSpec((local, HD), row),
            pl.BlockSpec((local, HD), row),
        ],
        out_specs=[pl.BlockSpec((local, GROUP * HD), lambda s, j: (s, j))]
        + [pl.BlockSpec((local, 2 * KVH * HD), row)] * parts,
        out_shape=[sds((rows, H * HD), BF16)] + [sds((rows, 2 * KVH * HD), BF16)] * parts,
        scratch_shapes=[pltpu.VMEM((full, local), F32)],
        cost_estimate=cost(20 * rows * full * H * HD, 8 * rows * H * HD, rows * full * H),
        name="attend_back",
    )(q, *slots, *slots, block_keys, block_mine, lse, grad, cosine, sine)


def out_project(attended, w_out, x, keep, gain, tile):
    rows, width = x.shape
    depth = attended.shape[1]

    def body(a_ref, w_ref, x_ref, k_ref, g_ref, m_ref, n_ref):
        mid = x_ref[...].astype(F32) + k_ref[...] * dot(a_ref[...], w_ref[...])
        inv = lax.rsqrt(jnp.mean(mid * mid, -1, keepdims=True) + EPS)
        m_ref[...] = mid
        n_ref[...] = (mid * inv * g_ref[...]).astype(BF16)

    return pl.pallas_call(
        body,
        grid=(rows // tile,),
        in_specs=[
            pl.BlockSpec((tile, depth), lambda i: (i, 0)),
            const_spec((depth, width)),
            pl.BlockSpec((tile, width), lambda i: (i, 0)),
            pl.BlockSpec((tile, 1), lambda i: (i, 0)),
            const_spec((1, width)),
        ],
        out_specs=[pl.BlockSpec((tile, width), lambda i: (i, 0))] * 2,
        out_shape=[sds((rows, width), F32), sds((rows, width), BF16)],
        cost_estimate=cost(2 * rows * depth * width, 2 * depth * width + 10 * rows * width),
        name="out_project",
    )(attended, w_out, x, keep, gain)


def gate_matmul(normed, w_gate, hidden, tile):
    rows, width = normed.shape

    def body(x_ref, w_ref, g_ref):
        g_ref[...] = dot(x_ref[...], w_ref[...]).astype(BF16)

    return pl.pallas_call(
        body,
        grid=(hidden // tile,),
        in_specs=[const_spec((rows, width)), pl.BlockSpec((width, tile), lambda j: (0, j))],
        out_specs=pl.BlockSpec((rows, tile), lambda j: (0, j)),
        out_shape=sds((rows, hidden), BF16),
        cost_estimate=cost(2 * rows * width * hidden, 2 * width * hidden + 2 * rows * hidden),
        name="gate_matmul",
    )(normed, w_gate)


def up_matmul(normed, w_up, start, gate, tile):
    rows, width = normed.shape
    hidden = gate.shape[1]

    def body(x_ref, w_ref, g_ref, u_ref, h_ref):
        up = dot(x_ref[...], w_ref[...])
        g = g_ref[...].astype(F32)
        u_ref[...] = up.astype(BF16)
        h_ref[...] = (g * jax.nn.sigmoid(g) * up).astype(BF16)

    return pl.pallas_call(
        body,
        grid=(hidden // tile,),
        in_specs=[
            const_spec((rows, width)),
            pl.BlockSpec((width, tile), lambda j: (0, start // tile + j)),
            pl.BlockSpec((rows, tile), lambda j: (0, j)),
        ],
        out_specs=[pl.BlockSpec((rows, tile), lambda j: (0, j))] * 2,
        out_shape=[sds((rows, hidden), BF16)] * 2,
        cost_estimate=cost(2 * rows * width * hidden, 2 * width * hidden + 6 * rows * hidden, rows * hidden),
        name="up_matmul",
    )(normed, w_up, gate)


def down_matmul(hidden, w_down, middle, keep):
    rows, depth = hidden.shape
    pieces, _, tile = w_down.shape

    def body(h_ref, w_ref, m_ref, k_ref, o_ref):
        o_ref[...] = (m_ref[...] + k_ref[...] * dot(h_ref[...], w_ref[0])).astype(BF16)

    return pl.pallas_call(
        body,
        grid=(pieces,),
        in_specs=[
            const_spec((rows, depth)),
            pl.BlockSpec((1, depth, tile), lambda i: (i, 0, 0)),
            pl.BlockSpec((rows, tile), lambda i: (0, i)),
            const_spec((rows, 1)),
        ],
        out_specs=pl.BlockSpec((rows, tile), lambda i: (0, i)),
        out_shape=sds((rows, pieces * tile), BF16),
        cost_estimate=cost(2 * rows * depth * pieces * tile, 2 * depth * pieces * tile + 2 * rows * depth),
        name="down_matmul",
    )(hidden, w_down, middle, keep)


def hidden_back(grad_mlp, w_down, gate, up, tile):
    rows, width = grad_mlp.shape
    pieces, hidden, part = w_down.shape

    def body(m_ref, w_ref, g_ref, u_ref, gg_ref, gu_ref):
        acc = dot(m_ref[:, :part], w_ref[0], NT)
        for i in range(1, pieces):
            acc = acc + dot(m_ref[:, i * part : (i + 1) * part], w_ref[i], NT)
        g = g_ref[...].astype(F32)
        u = u_ref[...].astype(F32)
        sig = jax.nn.sigmoid(g)
        gg_ref[...] = (acc * u * sig * (1.0 + g * (1.0 - sig))).astype(BF16)
        gu_ref[...] = (acc * g * sig).astype(BF16)

    return pl.pallas_call(
        body,
        grid=(hidden // tile,),
        in_specs=[
            const_spec((rows, width)),
            pl.BlockSpec((pieces, tile, part), lambda j: (0, j, 0)),
            pl.BlockSpec((rows, tile), lambda j: (0, j)),
            pl.BlockSpec((rows, tile), lambda j: (0, j)),
        ],
        out_specs=[pl.BlockSpec((rows, tile), lambda j: (0, j))] * 2,
        out_shape=[sds((rows, hidden), BF16)] * 2,
        cost_estimate=cost(2 * rows * width * hidden, 2 * width * hidden + 8 * rows * hidden, rows * hidden),
        name="hidden_back",
    )(grad_mlp, w_down, gate, up)


def mlp_back(grad_gate, grad_up, weights, tile):
    rows, hidden = grad_gate.shape
    width = weights.shape[0]

    def body(a_ref, b_ref, wa_ref, wb_ref, o_ref):
        o_ref[...] = dot(a_ref[...], wa_ref[...], NT) + dot(b_ref[...], wb_ref[...], NT)

    once = pl.Buffered(1)
    return pl.pallas_call(
        body,
        grid=(width // tile,),
        in_specs=[
            pl.BlockSpec((rows, hidden), lambda i: (0, 0), pipeline_mode=once),
            pl.BlockSpec((rows, hidden), lambda i: (0, 0), pipeline_mode=once),
            pl.BlockSpec((tile, hidden), lambda i: (i, 0)),
            pl.BlockSpec((tile, hidden), lambda i: (i, 1)),
        ],
        out_specs=pl.BlockSpec((rows, tile), lambda i: (0, i)),
        out_shape=sds((rows, width), F32),
        cost_estimate=cost(4 * rows * width * hidden, 4 * width * hidden + 4 * rows * hidden),
        name="mlp_back",
    )(grad_gate, grad_up, weights, weights)


def middle_back(grad_normed, middle, cotangent, keep, gain, w_out, tile):
    rows, width = middle.shape
    depth = w_out.shape[0]

    def body(n_ref, m_ref, c_ref, k_ref, g_ref, w_ref, gm_ref, gb_ref, ga_ref, gg_ref):
        mid = m_ref[...]
        inv = lax.rsqrt(jnp.mean(mid * mid, -1, keepdims=True) + EPS)
        unit = mid * inv
        grad = n_ref[...]
        u = grad * g_ref[...]
        gmid = c_ref[...].astype(F32) + inv * (u - unit * jnp.mean(u * unit, -1, keepdims=True))
        branch = (k_ref[...] * gmid).astype(BF16)
        gm_ref[...] = gmid
        gb_ref[...] = branch
        ga_ref[...] = dot(branch, w_ref[...], NT).astype(BF16)
        total = jnp.sum(grad * unit, 0, keepdims=True)

        @pl.when(pl.program_id(0) == 0)
        def _():
            gg_ref[...] = total

        @pl.when(pl.program_id(0) > 0)
        def _():
            gg_ref[...] += total

    row = lambda i: (i, 0)
    return pl.pallas_call(
        body,
        grid=(rows // tile,),
        in_specs=[
            pl.BlockSpec((tile, width), row),
            pl.BlockSpec((tile, width), row),
            pl.BlockSpec((tile, width), row),
            pl.BlockSpec((tile, 1), row),
            const_spec((1, width)),
            const_spec((depth, width)),
        ],
        out_specs=[
            pl.BlockSpec((tile, width), row),
            pl.BlockSpec((tile, width), row),
            pl.BlockSpec((tile, depth), row),
            const_spec((1, width)),
        ],
        out_shape=[sds((rows, width), F32), sds((rows, width), BF16), sds((rows, depth), BF16), sds((1, width), F32)],
        cost_estimate=cost(2 * rows * depth * width, 2 * depth * width + 18 * rows * width),
        name="middle_back",
    )(grad_normed, middle, cotangent, keep, gain, w_out)


def input_back(grad_q, grad_kv, weights, start, x, grad_middle, gain, tile):
    rows, width = x.shape
    depth_q, depth_kv = grad_q.shape[1], grad_kv.shape[1]

    def body(q_ref, kv_ref, wq_ref, wkv_ref, x_ref, m_ref, g_ref, o_ref, gg_ref):
        grad = dot(q_ref[...], wq_ref[...], NT) + dot(kv_ref[...], wkv_ref[...], NT)
        xin = x_ref[...].astype(F32)
        inv = lax.rsqrt(jnp.mean(xin * xin, -1, keepdims=True) + EPS)
        unit = xin * inv
        u = grad * g_ref[...]
        o_ref[...] = (m_ref[...] + inv * (u - unit * jnp.mean(u * unit, -1, keepdims=True))).astype(BF16)
        total = jnp.sum(grad * unit, 0, keepdims=True)

        @pl.when(pl.program_id(0) == 0)
        def _():
            gg_ref[...] = total

        @pl.when(pl.program_id(0) > 0)
        def _():
            gg_ref[...] += total

    row = lambda i: (i, 0)
    return pl.pallas_call(
        body,
        grid=(rows // tile,),
        in_specs=[
            pl.BlockSpec((tile, depth_q), row),
            pl.BlockSpec((tile, depth_kv), row),
            pl.BlockSpec((width, depth_q), lambda i: (0, start // depth_q), pipeline_mode=pl.Buffered(1)),
            pl.BlockSpec(
                (width, depth_kv), lambda i: (0, (start + depth_q) // depth_kv), pipeline_mode=pl.Buffered(1)
            ),
            pl.BlockSpec((tile, width), row),
            pl.BlockSpec((tile, width), row),
            const_spec((1, width)),
        ],
        out_specs=[pl.BlockSpec((tile, width), row), const_spec((1, width))],
        out_shape=[sds((rows, width), BF16), sds((1, width), F32)],
        cost_estimate=cost(2 * rows * width * (depth_q + depth_kv), 2 * width * (depth_q + depth_kv) + 10 * rows * width),
        name="input_back",
    )(grad_q, grad_kv, weights, weights, x, grad_middle, gain)


def weight_grad(side, chips, a_own, a_pair, b_own, b_pair, tile, total=None, first=0, into=None):
    rows, depth = a_own.shape
    width = b_own.shape[1]
    part = depth // (2 * len(chips))
    out_rows = depth // 2
    held = [] if into is None else [into]

    def body(side_ref, ao_ref, ap_ref, bo_ref, bp_ref, *refs):
        o_ref, to_ref, tp_ref = refs[len(held) :]

        @pl.when(pl.program_id(0) == 0)
        def _():
            for k, chip in enumerate(chips):
                at = pl.ds(pl.multiple_of((2 * chip + side_ref[0]) * part, part), part)
                own = slice(k * part, (k + 1) * part)
                to_ref[own, :] = ao_ref[:, at].T
                tp_ref[own, :] = ap_ref[:, at].T

        o_ref[...] = (dot(to_ref[...], bo_ref[...]) + dot(tp_ref[...], bp_ref[...])).astype(BF16)

    return pl.pallas_call(
        body,
        grid_spec=pltpu.PrefetchScalarGridSpec(
            num_scalar_prefetch=1,
            grid=(width // tile,),
            in_specs=[
                pl.BlockSpec((rows, depth), lambda j, _: (0, 0), pipeline_mode=pl.Buffered(1)),
                pl.BlockSpec((rows, depth), lambda j, _: (0, 0), pipeline_mode=pl.Buffered(1)),
                pl.BlockSpec((rows, tile), lambda j, _: (0, j)),
                pl.BlockSpec((rows, tile), lambda j, _: (0, j)),
            ]
            + [pl.BlockSpec(memory_space=pl.ANY)] * len(held),
            out_specs=pl.BlockSpec((out_rows, tile), lambda j, _: (0, first + j)),
            scratch_shapes=[pltpu.VMEM((out_rows, rows), BF16)] * 2,
        ),
        out_shape=sds((out_rows, width if total is None else total), BF16),
        input_output_aliases={5: 0} if held else {},
        cost_estimate=cost(4 * rows * out_rows * width, 2 * out_rows * width + 4 * rows * width + 4 * rows * depth),
        name="weight_grad",
    )(side, a_own, a_pair, b_own, b_pair, *held)


def on_device(
    layer_input,
    cotangent,
    positions,
    block_ids,
    skip_mask,
    attn_gain,
    w_query,
    w_key,
    w_value,
    w_out,
    mlp_gain,
    w_gate,
    w_up,
    w_down,
):
    seqs, local, width = layer_input.shape
    rows = seqs * local
    fsdp = lax.axis_size("fsdp")
    parts = lax.axis_size("ulysses")
    place = lax.axis_index("ulysses")
    side = lax.rem(lax.axis_index("fsdp"), 2).astype(jnp.int32).reshape(1)
    chips = fsdp // 2
    ring = [0, 1, 3, 2] if chips == 4 else list(range(chips))
    groups = [[2 * chip + core for chip in ring] for core in range(2)]
    pairs = [(i, i ^ 1) for i in range(fsdp)]
    ahead = min(parts - 1, -(-(BLOCK - 1) // local))
    query_width, pair_width = H * HD, KVH * HD
    hidden_width = w_gate.shape[1]
    tile = 512

    def after(v, *others):
        return lax.optimization_barrier((v,) + others)[0]

    def gather(v, tiled=True):
        return lax.all_gather(v, "fsdp", axis=0, tiled=tiled)

    def swap(v):
        return lax.ppermute(v, "fsdp", pairs)

    def scatter(v):
        return lax.psum_scatter(
            v, "fsdp", scatter_dimension=0, tiled=True, axis_index_groups=groups
        )

    def finish(v):
        return lax.psum(v, "ulysses")

    middle_part = parts // 2
    hops = [
        ([(d, d + 1), (parts - 1 - d, parts - 2 - d)], None) for d in range(middle_part - 1)
    ]
    hops.append(([(middle_part - 1, middle_part), (middle_part, middle_part - 1)], None))
    hops += [
        ([(d, d - 1), (parts - 1 - d, parts - d)], (place == d - 1) | (place == parts - d))
        for d in range(middle_part - 1, 0, -1)
    ]
    under_way = []

    def add(a, b):
        return (a.astype(F32) + b.astype(F32)).astype(BF16)

    def tick(new, *gates):
        for chunk in under_way:
            came, takes = chunk["came"], hops[chunk["hop"] - 1][1]
            chunk["v"] = add(chunk["v"], came) if takes is None else jnp.where(takes, came, chunk["v"])
        for out, k, v in new:
            under_way.append({"out": out, "k": k, "v": v, "hop": 0})
        held = lax.optimization_barrier(tuple(c["v"] for c in under_way) + gates)
        for chunk, v in zip(list(under_way), held):
            chunk["v"] = v
            if chunk["hop"] == len(hops):
                chunk["out"][chunk["k"]] = v
                under_way.remove(chunk)
            else:
                chunk["came"] = lax.ppermute(v, "ulysses", hops[chunk["hop"]][0])
                chunk["hop"] += 1
        return held[0]

    def chunks(v, count):
        out, step = {}, v.shape[0] // count
        return out, [(out, k, v[k * step : (k + 1) * step]) for k in range(count)]

    def joined(out):
        return jnp.concatenate([out[k] for k in range(len(out))], 0)

    def grad_of(*operands, **where):
        return weight_grad(side, ring, *operands, tile, **where)

    def spread(v):
        ups, held = [], v
        for r in range(1, parts):
            held = lax.ppermute(held, "ulysses", [(i, i + 1) for i in range(r - 1, parts - 1)])
            ups.append(held)
        slots = [v] + ups
        for i in range(1, ahead + 1):
            down = lax.ppermute(v, "ulysses", [(z + i, z) for z in range(parts - i)])
            slots[parts - i] = jnp.where(place >= parts - i, slots[parts - i], down)
        return slots

    def collect(slots):
        total = slots[0].astype(F32)
        ups = [
            lax.ppermute(slots[parts - i], "ulysses", [(z, z + i) for z in range(parts - i)])
            for i in range(1, ahead + 1)
        ]
        held = slots[parts - 1]
        for r in range(parts - 1, 0, -1):
            came = lax.ppermute(held, "ulysses", [(i, i - 1) for i in range(r, parts)])
            if r > 1:
                held = yield add(slots[r - 1], came)
            else:
                for up in ups:
                    total = total + up.astype(F32)
                yield total + came.astype(F32)

    gains = lax.all_gather(jnp.stack([attn_gain, mlp_gain]), "fsdp", axis=1, tiled=True).astype(F32)
    gain_one, gain_two = gains[0:1], gains[1:2]
    att_full = gather(jnp.concatenate([w_out, w_query, w_key, w_value], 1))
    mlp_full = gather(after(jnp.concatenate([w_gate, w_up], 1), att_full))

    first_sum = finish(w_key)
    x = layer_input.reshape(rows, width)
    xf = x.astype(F32)
    inv_one = lax.rsqrt(jnp.mean(xf * xf, -1, keepdims=True) + EPS)
    normed_one = (xf * inv_one * gain_one).astype(BF16)
    keep = jnp.repeat((1 - skip_mask).astype(F32), local)[:, None]
    cot = cotangent.reshape(rows, width)
    grad_mlp = (keep * cot.astype(F32)).astype(BF16)

    half = HD // 2
    frequency = jnp.exp(jnp.arange(half, dtype=F32) * (-2.0 * math.log(10000.0) / HD))
    angles = positions.reshape(rows, 1).astype(F32) * frequency
    cosine = jnp.concatenate([jnp.cos(angles)] * 2, -1)
    sine = jnp.sin(angles)
    sine = jnp.concatenate([-sine, sine], -1)
    by_part = block_ids.reshape(seqs, parts, local)
    block_mine = lax.dynamic_slice_in_dim(by_part, place, 1, 1)
    order = lax.rem(place - jnp.arange(parts) + parts, parts)
    block_keys = jnp.take(by_part, order, 1).reshape(seqs, parts * local, 1)

    query, kv = project(normed_one, att_full, width, cosine, sine)
    slots = spread(kv)
    one_pair, mlp_pair = swap(normed_one), swap(grad_mlp)
    attended, lse = attend(query, slots, block_keys, block_mine, seqs)
    middle, normed_two = out_project(attended, att_full, x, keep, gain_two, local)
    gate = gate_matmul(normed_two, mlp_full, hidden_width, tile)
    down_full = gather(after(w_down, mlp_full, normed_two), False)
    two_pair, att_pair = swap(normed_two), swap(attended)
    up, hidden = up_matmul(normed_two, mlp_full, hidden_width, gate, tile)

    hidden_pair = swap(hidden)
    down_part = grad_of(grad_mlp, mlp_pair, hidden, hidden_pair)
    down_sum = scatter(down_part)
    grad_gate, grad_up = hidden_back(after(grad_mlp, down_part), down_full, gate, up, tile)
    gate_pair, up_pair = swap(grad_gate), swap(grad_up)
    grad_normed_two = mlp_back(grad_gate, grad_up, mlp_full, 256)
    gate_part = grad_of(normed_two, two_pair, after(grad_gate, grad_normed_two), gate_pair)
    gate_sum = scatter(after(gate_part, down_sum))
    down_all = finish(after(down_sum, gate_part, first_sum))
    grad_middle, grad_branch, grad_attended, grad_gain_two = middle_back(
        after(grad_normed_two, gate_part), middle, cot, keep, gain_two, att_full, local
    )
    branch_pair = swap(grad_branch)
    grad_query, *grad_slots = attend_back(
        query, slots, block_keys, block_mine, lse, grad_attended, cosine, sine, seqs
    )
    query_pair = swap(grad_query)
    collecting = collect(grad_slots)
    kv_held = next(collecting)
    up_part = grad_of(normed_two, two_pair, after(grad_up, grad_query), up_pair)
    up_sum = scatter(after(up_part, gate_sum))
    columns = query_width + width
    att_part = grad_of(
        attended, att_pair, after(grad_branch, up_part, gate_sum), branch_pair, total=columns, first=query_width // tile
    )
    gate_all = finish(after(gate_sum, up_part, down_all))
    att_part = grad_of(
        normed_one, one_pair, after(grad_query, down_all, kv_held), query_pair, total=columns, into=att_part
    )
    for _ in range(parts - 3):
        kv_held = collecting.send(kv_held)
    att_sum = scatter(after(att_part, up_sum))
    up_all, fresh = chunks(up_sum, 2)
    token = tick(fresh[:1], att_part, kv_held, gate_all)
    grad_kv = collecting.send(after(kv_held, token))
    output = down_matmul(after(hidden, token), down_full, middle, keep)
    token = tick(fresh[1:], output)
    out_down = after(down_all, token).astype(F32).T
    att_all, fresh = chunks(att_sum, 2)
    token = tick(fresh[:1])
    token = tick(fresh[1:])
    grad_kv = after(grad_kv, token)
    grad_key = grad_kv[:, :pair_width].reshape(rows, KVH, HD)
    turned = grad_key * sine[:, None, :]
    turned = jnp.concatenate([turned[..., half:], turned[..., :half]], -1)
    grad_key = (grad_key * cosine[:, None, :] + turned).reshape(rows, pair_width)
    grad_kv = jnp.concatenate([grad_key, grad_kv[:, pair_width:]], 1).astype(BF16)
    kv_pair = swap(grad_kv)
    kv_part = grad_of(normed_one, one_pair, after(grad_kv, token), kv_pair)
    grad_input, grad_gain_one = input_back(
        grad_query, after(grad_kv, kv_part, out_down), att_full, width, x, grad_middle, gain_one, local
    )
    gain_grads = jnp.concatenate([grad_gain_one, grad_gain_two], 0)
    gain_grads = (gain_grads + swap(gain_grads)).reshape(2, chips, 2, width // fsdp)
    gain_grads = lax.dynamic_index_in_dim(gain_grads, side[0], 2, False)
    gain_grads = jnp.stack([gain_grads[:, chip] for chip in ring], 1).reshape(2, width // 2)
    gain_part = jnp.pad(gain_grads.T, ((0, 0), (0, HD - 2))).astype(BF16)
    kv_sum = scatter(after(jnp.concatenate([kv_part, gain_part], 1), att_sum))
    out_gate = after(gate_all, token).astype(F32)
    kv_sums, fresh = chunks(kv_sum, 1)
    token = tick(fresh)
    while under_way:
        token = tick([])
    out_up = joined(up_all).astype(F32)
    att_all, kv_sums = joined(att_all), joined(kv_sums)
    out_query = att_all[:, :query_width].astype(F32)
    out_out = att_all[:, query_width:].astype(F32)
    out_key = kv_sums[:, :pair_width].astype(F32)
    out_value = kv_sums[:, pair_width : 2 * pair_width].astype(F32)
    out_gains = kv_sums[:, 2 * pair_width : 2 * pair_width + 2].astype(F32).T + 0.0 * first_sum[0, 0].astype(F32)
    return (
        output.reshape(layer_input.shape),
        grad_input.reshape(layer_input.shape),
        out_gains[0],
        out_query,
        out_key,
        out_value,
        out_out,
        out_gains[1],
        out_gate,
        out_up,
        out_down,
    )


def solution(mesh):
    return jax.shard_map(
        on_device,
        mesh=mesh,
        in_specs=(
            P("fsdp", "ulysses", None),
            P("fsdp", "ulysses", None),
            P("fsdp", "ulysses"),
            P("fsdp", None),
            P("fsdp"),
            P("fsdp"),
            P("fsdp", None),
            P("fsdp", None),
            P("fsdp", None),
            P("fsdp", None),
            P("fsdp"),
            P("fsdp", None),
            P("fsdp", None),
            P(None, "fsdp"),
        ),
        out_specs=(
            P("fsdp", "ulysses", None),
            P("fsdp", "ulysses", None),
            P("fsdp"),
            P("fsdp", None),
            P("fsdp", None),
            P("fsdp", None),
            P("fsdp", None),
            P("fsdp"),
            P("fsdp", None),
            P("fsdp", None),
            P(None, "fsdp"),
        ),
        check_vma=False,
    )
```
